32 devices in a mesh: rep: 2 (over core), shard: 16 (over z, y, x).
Axes of the slice: x: 2, y: 2, z: 4, core: 2. Of those that a mesh axis runs over, the one named last changes fastest.
Arguments:
- z_state: float32 [8192, 128], P('shard'), may hold values from -12 to 12
- n_state: float32 [8192, 128], P('shard'), may hold values from 0.1 to 10
- tile_values: bfloat16 [8192, 128, 128], P(('rep', 'shard')), may hold values from -0.29882812 to 0.29882812
- tile_block: int32 [8192], P(('rep', 'shard')), may hold values from 0 to 8191, as said below
- tile_group: int32 [8192], P(('rep', 'shard')), may hold values from 0 to 7, as said below
- labels: int32 [256, 128], P(('rep', 'shard')), may hold values 0 or 1
Outputs:
- margins: float32 [256, 128], P(('rep', 'shard'))
- new_z: float32 [8192, 128], P('shard', 'rep')
- new_n: float32 [8192, 128], P('shard', 'rep')
- new_w: float32 [8192, 128], P('shard', 'rep')
The draws below stay inside these ranges and needn't reach their ends.
Inputs may be any that keep to these rules, and one draw needn't show every extreme that they name: `tile_block`: block b belongs to server shard b // 512. Among the 256 tiles of one device, at most 18 belong to one server shard; in every draw one server shard gets exactly 18 tiles from every device. `tile_group`: each row group of a device is named by exactly 32 of its tiles.
All inputs are finite; a program needn't handle non-finite values. No bound on the sum of `labels` on one device may be relied on, other than what follows from the above.
Results may differ from the reference program's by a relative error of at most 0.0049.
Values may be sent and summed in bfloat16 or wider, within the bound.
No kernel may reach another device: no remote copies, remote signals or barrier semaphores. Data moves between devices by JAX's collectives and lax.ppermute only.
A program may use at most 64 MiB of HBM per device.

```python
import math
import jax
import jax.numpy as jnp
from jax import lax

LANE = 128
BLK_DEV = 512
TILE_DEV = 256
GROUPS = 8
CAP = 18
BLOCKS = 8192
TILES = 8192
ROWS = 256
N_SHARD = 16
DEVICES = 32


def routing(key):
    hot_shard = jax.random.randint(jax.random.fold_in(key, 7), (), 0, N_SHARD).astype(jnp.int32)

    def one_worker(worker):
        wkey = jax.random.fold_in(key, worker + 11)
        others = jax.random.permutation(jax.random.fold_in(wkey, 1), N_SHARD - 1).astype(jnp.int32)
        position = jnp.arange(TILE_DEV, dtype=jnp.int32)
        index = jnp.maximum(position - CAP, 0) % (N_SHARD - 1)
        owner = jnp.where(position < CAP, hot_shard, (hot_shard + 1 + others[index]) % N_SHARD)
        hot_local = jax.random.randint(jax.random.fold_in(wkey, 2), (TILE_DEV,), 0, 2).astype(jnp.int32)
        any_local = jax.random.randint(jax.random.fold_in(wkey, 3), (TILE_DEV,), 0, BLK_DEV).astype(jnp.int32)
        local = jnp.where(position < CAP, hot_local, any_local)
        order = jax.random.permutation(jax.random.fold_in(wkey, 4), TILE_DEV).astype(jnp.int32)
        block = (owner * BLK_DEV + local)[order]
        group = jax.random.permutation(jax.random.fold_in(wkey, 5), TILE_DEV).astype(jnp.int32) % GROUPS
        return (block.astype(jnp.int32), group.astype(jnp.int32))
    blocks, groups = jax.vmap(one_worker)(jnp.arange(DEVICES, dtype=jnp.int32))
    return (blocks.reshape(-1), groups.reshape(-1))


def draw_tile_block(key, part):
    return routing(key)[0]


def draw_tile_group(key, part):
    return routing(key)[1]


def place_ends(values, rng, smallest, high):
    longest = values.shape.index(max(values.shape))
    spots = []
    for shift in (0, 1):
        where = [jax.random.randint(jax.random.fold_in(rng, axis), (), 0, length) for axis, length in enumerate(values.shape)]
        where[longest] = (where[longest] + shift) % values.shape[longest]
        spots.append(tuple(where))
    return values.at[spots[0]].set(smallest).at[spots[1]].set(high)


def levels(rng, shape, cuts, smallest, high):
    def one(axis_at, parts):
        draws = jax.random.uniform(jax.random.fold_in(jax.random.fold_in(rng, 6), axis_at), (parts,), jnp.float32, smallest / len(cuts), high / len(cuts))
        return jnp.repeat(jnp.exp(draws), shape[axis_at] // parts).reshape((-1,) + (1,) * (len(shape) - axis_at - 1))

    gain = one(*cuts[0])
    for cut in cuts[1:]:
        gain = gain * one(*cut)
    return gain


def normal_values(rng, extent, spread, most, split=(), kind=jnp.bfloat16):
    factor_of = levels(rng, extent, split, -0.22, 0.18) if split else 1.0
    entries = jax.random.normal(rng, extent, jnp.float32) * spread * factor_of
    return jnp.minimum(jnp.maximum(entries, -most), most).astype(kind)


def setup_inputs(seed: int = 0) -> dict:
    streams_of = jax.random.split(jax.random.key(seed), 7)
    return {
        "z_state": normal_values(streams_of[0], (BLOCKS, LANE), 3.0, 12.0, ((0, 16),), jnp.float32),
        "n_state": jnp.clip(jnp.exp(math.log(10.0) - 4.6051702 * jax.random.uniform(streams_of[1], (BLOCKS, LANE), jnp.float32) ** levels(streams_of[1], (BLOCKS, LANE), ((0, 16),), -0.2, 0.2)), 0.1, 10.0),
        "tile_values": normal_values(streams_of[2], (TILES, LANE, LANE), 0.05, 0.29882812, ((0, 32),)),
        "tile_block": draw_tile_block(jax.random.fold_in(streams_of[6], 71), 0),
        "tile_group": draw_tile_group(jax.random.fold_in(streams_of[6], 71), 0),
        "labels": place_ends((jax.random.randint(streams_of[5], (ROWS, LANE), 0, 4) < 1).astype(jnp.int32), jax.random.fold_in(streams_of[5], 1), 0, 1),
    }


rate_alpha = 0.5
rate_beta = 1.0
lasso_weight = 0.5
ridge_weight = 1.0

def shrink(z_acc, n_acc):
    soft = z_acc - jnp.clip(z_acc, -lasso_weight, lasso_weight)
    return -soft / ((rate_beta + jnp.sqrt(n_acc)) / rate_alpha + ridge_weight)

def reference(z_state, n_state, tile_values, tile_block, tile_group, labels):
    w_old = shrink(z_state, n_state)
    w_pull = w_old.astype(jnp.bfloat16)
    values = tile_values.reshape(DEVICES, TILE_DEV, LANE, LANE)
    blocks = tile_block.reshape(DEVICES, TILE_DEV)
    groups = tile_group.reshape(DEVICES, TILE_DEV)
    clicks = labels.reshape(DEVICES, GROUPS, LANE)

    def worker(items):
        vals, blk, grp, lab = items
        wide = vals.astype(jnp.float32)
        pulled = w_pull[blk].astype(jnp.float32)
        contrib = jnp.einsum('tef,tf->te', wide, pulled, precision=lax.Precision.HIGHEST)
        member = (grp[None, :] == jnp.arange(GROUPS, dtype=jnp.int32)[:, None]).astype(jnp.float32)
        rows = jnp.dot(member, contrib, precision=lax.Precision.HIGHEST)
        resid = (jax.nn.sigmoid(rows) - lab.astype(jnp.float32)).astype(jnp.bfloat16)
        per_tile = resid[grp].astype(jnp.float32)
        grads = jnp.einsum('tef,te->tf', wide, per_tile, precision=lax.Precision.HIGHEST)
        return (rows, grads)
    rows, grads = lax.map(worker, (values, blocks, groups, clicks))
    total = jnp.zeros((BLOCKS, LANE), jnp.float32).at[tile_block].add(grads.reshape(-1, LANE))
    sigma = (jnp.sqrt(n_state + total * total) - jnp.sqrt(n_state)) / rate_alpha
    new_z = z_state + total - sigma * w_old
    new_n = n_state + total * total
    new_w = shrink(new_z, new_n)
    return (rows.reshape(ROWS, LANE), new_z, new_n, new_w)
```

```python
import functools

import jax
import jax.numpy as jnp
from jax import lax
from jax.experimental import pallas as pl
from jax.experimental.pallas import tpu as pltpu
from jax.sharding import PartitionSpec as P

rate_alpha = 0.5
rate_beta = 1.0
lasso_weight = 0.5
ridge_weight = 1.0

f32, bf16, i32 = jnp.float32, jnp.bfloat16, jnp.int32
VMEM = pl.BlockSpec(memory_space=pltpu.VMEM)
SMEM = pl.BlockSpec(memory_space=pltpu.SMEM)


def shrink(z_acc, n_acc):
    soft = z_acc - jnp.clip(z_acc, -lasso_weight, lasso_weight)
    return -soft / ((rate_beta + jnp.sqrt(n_acc)) / rate_alpha + ridge_weight)


def iota(shape, dim):
    return lax.broadcasted_iota(i32, shape, dim)


def before(size):
    return (iota((size, size), 0) < iota((size, size), 1)).astype(bf16)


def slot_ids(asked, cap, first, blk):
    parts = asked.shape[1]
    tri = before(128)
    count = None
    picked = None
    for part in range(parts):
        local = asked[:, part, :] - first
        valid = (local >= 0) & (local < blk)
        ones = valid.astype(f32)
        rank = jnp.dot(ones.astype(bf16), tri, preferred_element_type=f32)
        total = jnp.sum(ones, axis=1, keepdims=True)
        if count is not None:
            rank = rank + count
            total = total + count
        count = total
        place = jnp.where(valid, rank.astype(i32), -1)[:, None, :]
        value = (local + 1).astype(f32)[:, None, :]
        shape = (place.shape[0], cap, 128)
        hit = jnp.broadcast_to(place, shape) == iota(shape, 1)
        here = jnp.where(hit, jnp.broadcast_to(value, shape), 0.0)
        picked = here if picked is None else picked + here
    return jnp.sum(picked, axis=2, keepdims=True).astype(i32) - 1


def one_hot_rows(ids, blk):
    rows, cap, _ = ids.shape
    shape = (rows, cap, blk)
    hot = (jnp.broadcast_to(ids, shape) == iota(shape, 2)).astype(f32).astype(bf16)
    return hot.reshape(rows * cap, blk)


def route_kernel(shards, groups, cap, blk, block_ref, group_ref, order_ref, take_ref, put_ref):
    tiles = block_ref.shape[1]
    slots = shards * cap
    tri = before(tiles)
    owner = block_ref[...] // blk
    group = group_ref[...]
    mine = jnp.broadcast_to(owner, (shards, tiles)) == iota((shards, tiles), 0)
    rank = jnp.dot(mine.astype(f32).astype(bf16), tri, preferred_element_type=f32)
    rank = jnp.sum(jnp.where(mine, rank, 0.0), axis=0, keepdims=True)
    inside = jnp.broadcast_to(group, (groups, tiles)) == iota((groups, tiles), 0)
    place = jnp.dot(inside.astype(f32).astype(bf16), tri, preferred_element_type=f32)
    place = place + (iota((groups, tiles), 0) * (tiles // groups)).astype(f32)
    place = jnp.sum(jnp.where(inside, place, 0.0), axis=0, keepdims=True).astype(i32)
    move = (jnp.broadcast_to(place, (tiles, tiles)) == iota((tiles, tiles), 0)).astype(f32)
    slot = owner.astype(f32) * cap + rank
    column = jnp.sum(move * slot, axis=1, keepdims=True).astype(i32)
    take_ref[...] = (jnp.broadcast_to(column, (tiles, slots)) == iota((tiles, slots), 1)).astype(f32).astype(bf16)
    row = iota((8, tiles), 0)
    facts = jnp.where(
        row == 0,
        jnp.broadcast_to(owner.astype(f32), (8, tiles)),
        jnp.where(row == 1, jnp.broadcast_to(rank, (8, tiles)), iota((8, tiles), 1).astype(f32)),
    )
    facts = lax.dot_general(
        facts.astype(bf16), move.astype(bf16), (((1,), (1,)), ((), ())), preferred_element_type=f32
    )
    order_ref[...] = facts[2:3].astype(i32)
    target = (facts[0:1] * cap + facts[1:2]).astype(i32)
    put_ref[...] = (jnp.broadcast_to(target, (slots, tiles)) == iota((slots, tiles), 0)).astype(f32).astype(bf16)


def answer_kernel(shards, cap, asked_ref, z_ref, n_ref, answer_ref):
    blk, lane = z_ref.shape
    me = lax.axis_index("shard")
    rep = lax.axis_index("rep")
    w_pull = shrink(z_ref[...], n_ref[...]).astype(bf16)
    asked = asked_ref[pl.ds(rep * shards, shards)]
    hot = one_hot_rows(slot_ids(asked, cap, me * blk, blk), blk)
    rows = jnp.dot(hot, w_pull, preferred_element_type=f32)
    answer_ref[...] = rows.astype(bf16).reshape(shards, cap, lane)


def state_kernel(cap, asked_ref, z_ref, n_ref, hot_ref, zt_ref, nt_ref):
    blk, lane = z_ref.shape
    half = zt_ref.shape[0]
    me = lax.axis_index("shard")
    rep = lax.axis_index("rep")
    hot_ref[...] = one_hot_rows(slot_ids(asked_ref[...], cap, me * blk, blk), blk)
    zt = z_ref[...].T
    nt = n_ref[...].T
    zt_ref[...] = jnp.where(rep == 0, zt[:half], zt[half:])
    nt_ref[...] = jnp.where(rep == 0, nt[:half], nt[half:])


def worker_kernel(
    shards, cap, order_ref, answer_ref, take_ref, put_ref, labels_ref, tile_ref, margin_ref, out_ref, w_ref, sum_ref, grad_ref
):
    tiles, lane, _ = tile_ref.shape
    groups = labels_ref.shape[0]
    each = tiles // groups
    slots = shards * cap
    w_ref[...] = jnp.dot(take_ref[...], answer_ref[...].reshape(slots, lane), preferred_element_type=f32)
    for g in range(groups):
        def add(j, acc):
            p = g * each + j
            return acc + tile_ref[order_ref[0, p]].astype(f32) * w_ref[pl.ds(p, 1), :]

        sum_ref[g] = lax.fori_loop(0, each, add, jnp.zeros((lane, lane), f32), unroll=8)
    margins = jnp.concatenate([jnp.sum(sum_ref[g], axis=1).reshape(1, lane) for g in range(groups)], axis=0)
    margin_ref[...] = margins
    resid = (jax.nn.sigmoid(margins) - labels_ref[...].astype(f32)).astype(bf16)
    for g in range(groups):
        row = resid[g : g + 1]
        for j in range(0, each, 2):
            p = g * each + j
            pair = jnp.concatenate([tile_ref[order_ref[0, p]], tile_ref[order_ref[0, p + 1]]], axis=1)
            both = jnp.dot(row, pair, preferred_element_type=f32)
            grad_ref[p : p + 1, :] = both[:, :lane]
            grad_ref[p + 1 : p + 2, :] = both[:, lane:]
    sent = jnp.dot(put_ref[...], grad_ref[...].astype(bf16), preferred_element_type=f32)
    half = lane // 2
    out_ref[:shards] = sent[:, :half].astype(bf16).reshape(shards, cap, half)
    out_ref[shards:] = sent[:, half:].astype(bf16).reshape(shards, cap, half)


def update_kernel(incoming_ref, hot_ref, zt_ref, nt_ref, z_out, n_out, w_out):
    sources, cap, half = incoming_ref.shape
    total = lax.dot_general(
        incoming_ref[...].reshape(sources * cap, half),
        hot_ref[...],
        (((0,), (0,)), ((), ())),
        preferred_element_type=f32,
    )
    z_state = zt_ref[...]
    n_state = nt_ref[...]
    w_old = shrink(z_state, n_state)
    new_n = n_state + total * total
    sigma = (jnp.sqrt(new_n) - jnp.sqrt(n_state)) / rate_alpha
    new_z = z_state + total - sigma * w_old
    z_out[...] = new_z
    n_out[...] = new_n
    w_out[...] = shrink(new_z, new_n)


def call(kernel, out, specs, scratch=(), limit=16 << 20):
    return pl.pallas_call(
        kernel,
        out_shape=out,
        in_specs=specs,
        out_specs=jax.tree.map(lambda _: VMEM, out),
        scratch_shapes=list(scratch),
        compiler_params=pltpu.CompilerParams(vmem_limit_bytes=limit),
    )


def body(z_state, n_state, tile_values, tile_block, tile_group, labels):
    blk, lane = z_state.shape
    tiles = tile_block.shape[0]
    groups = labels.shape[0]
    shards = lax.axis_size("shard")
    reps = lax.axis_size("rep")
    half = lane // reps
    need = max(4, (tiles + shards - 2) // (shards - 1))
    cap = (need + 7) // 8 * 8
    slots = shards * cap
    axes = ("rep", "shard")
    shape = jax.ShapeDtypeStruct

    raw = jnp.broadcast_to(tile_block.reshape(1, tiles // 128, 128), (reps * shards, tiles // 128, 128))
    asked = lax.all_to_all(raw, axes, split_axis=0, concat_axis=0, tiled=True)
    order, take, put = call(
        functools.partial(route_kernel, shards, groups, cap, blk),
        (shape((1, tiles), i32), shape((tiles, slots), bf16), shape((slots, tiles), bf16)),
        [VMEM, VMEM],
    )(tile_block.reshape(1, tiles), tile_group.reshape(1, tiles))
    answer = call(
        functools.partial(answer_kernel, shards, cap), shape((shards, cap, lane), bf16), [VMEM] * 3
    )(asked, z_state, n_state)
    answer = lax.all_to_all(answer, "shard", split_axis=0, concat_axis=0, tiled=True)
    hot, zt, nt = call(
        functools.partial(state_kernel, cap),
        (shape((reps * slots, blk), bf16), shape((half, blk), f32), shape((half, blk), f32)),
        [VMEM] * 3,
    )(asked, z_state, n_state)
    margins, outgoing = call(
        functools.partial(worker_kernel, shards, cap),
        (shape((groups, lane), f32), shape((reps * shards, cap, half), bf16)),
        [SMEM] + [VMEM] * 5,
        [pltpu.VMEM((tiles, lane), f32), pltpu.VMEM((groups, lane, lane), f32), pltpu.VMEM((tiles, lane), f32)],
    )(order, answer, take, put, labels, tile_values)
    incoming = lax.all_to_all(outgoing, axes, split_axis=0, concat_axis=0, tiled=True)
    outs = call(update_kernel, (shape((half, blk), f32),) * 3, [VMEM] * 4)(incoming, hot, zt, nt)
    return (margins,) + tuple(o.T for o in outs)


def solution(mesh):
    placed = (
        P("shard", None),
        P("shard", None),
        P(("rep", "shard"), None, None),
        P(("rep", "shard")),
        P(("rep", "shard")),
        P(("rep", "shard"), None),
    )
    return jax.shard_map(
        body,
        mesh=mesh,
        in_specs=placed,
        out_specs=(
            P(("rep", "shard"), None),
            P("shard", "rep"),
            P("shard", "rep"),
            P("shard", "rep"),
        ),
        check_vma=False,
    )
```

```python
import functools

import jax
import jax.numpy as jnp
from jax import lax
from jax.experimental import pallas as pl
from jax.experimental.pallas import tpu as pltpu
from jax.sharding import PartitionSpec as P

rate_alpha = 0.5
rate_beta = 1.0
lasso_weight = 0.5
ridge_weight = 1.0

f32, bf16, i32 = jnp.float32, jnp.bfloat16, jnp.int32
VMEM = pl.BlockSpec(memory_space=pltpu.VMEM)
SMEM = pl.BlockSpec(memory_space=pltpu.SMEM)
HBM = pl.BlockSpec(memory_space=pltpu.HBM)
INNER = 4


def shrink(z_acc, n_acc):
    soft = z_acc - jnp.clip(z_acc, -lasso_weight, lasso_weight)
    return -soft / ((rate_beta + jnp.sqrt(n_acc)) / rate_alpha + ridge_weight)


def iota(shape, dim):
    return lax.broadcasted_iota(i32, shape, dim)


def mask(hit):
    return hit.astype(f32).astype(bf16)


def before(size):
    return mask(iota((size, size), 0) < iota((size, size), 1))


def pull_kernel(z_hbm, n_hbm, pull_ref, z_ref, n_ref, sem):
    z_copy = pltpu.make_async_copy(z_hbm, z_ref, sem.at[0])
    n_copy = pltpu.make_async_copy(n_hbm, n_ref, sem.at[1])
    z_copy.start()
    n_copy.start()
    z_copy.wait()
    n_copy.wait()
    pull_ref[...] = shrink(z_ref[...], n_ref[...]).astype(bf16)


def route_kernel(shards, groups, cap, room, relative, blk, block_ref, group_ref, order_ref, take_ref, put_ref, code_ref):
    tiles = block_ref.shape[1]
    outers = shards // INNER
    base = lax.axis_index("shard") // INNER if relative else 0
    tri = before(tiles)
    block = block_ref[...]
    owner = block // blk
    local = block - owner * blk + 1
    group = group_ref[...]

    def rank_in(key, count):
        same = jnp.broadcast_to(key, (count, tiles)) == iota((count, tiles), 0)
        rank = jnp.dot(mask(same), tri, preferred_element_type=f32)
        return jnp.sum(jnp.where(same, rank, 0.0), axis=0, keepdims=True)

    outer = (owner // INNER) ^ base
    answer_rank = rank_in(outer, outers)
    send_rank = rank_in(owner, shards)
    place = (group * (tiles // groups)).astype(f32) + rank_in(group, groups)
    move = (jnp.broadcast_to(place.astype(i32), (tiles, tiles)) == iota((tiles, tiles), 0)).astype(f32)
    slot = outer.astype(f32) * room + answer_rank
    column = jnp.sum(move * slot, axis=1, keepdims=True).astype(i32)
    take_ref[...] = mask(jnp.broadcast_to(column, (tiles, outers * room)) == iota((tiles, outers * room), 1))
    row = iota((8, tiles), 0)
    facts = jnp.where(
        row == 0,
        jnp.broadcast_to(owner.astype(f32), (8, tiles)),
        jnp.where(row == 1, jnp.broadcast_to(send_rank, (8, tiles)), iota((8, tiles), 1).astype(f32)),
    )
    facts = lax.dot_general(
        facts.astype(bf16), move.astype(bf16), (((1,), (1,)), ((), ())), preferred_element_type=f32
    )
    order_ref[...] = facts[2:3].astype(i32)
    target = (facts[0:1] * cap + facts[1:2]).astype(i32)
    put_ref[...] = mask(jnp.broadcast_to(target, (shards * cap, tiles)) == iota((shards * cap, tiles), 0))
    number = jnp.sum(move * local.astype(f32), axis=1, keepdims=True).astype(i32)
    lane = code_ref.shape[1]
    at = iota((tiles, lane), 1) - lane // 2
    low = jnp.broadcast_to((number % 256).astype(f32), (tiles, lane))
    high = jnp.broadcast_to((number // 256).astype(f32), (tiles, lane))
    code_ref[...] = jnp.where(at == 0, low, jnp.where(at == 1, high, 0.0)).astype(bf16)


def answer_kernel(asked_count, room, *refs):
    asked_refs = refs[:asked_count]
    table_refs = refs[asked_count : asked_count + INNER]
    out_refs = refs[asked_count + INNER :]
    blk, lane = table_refs[0].shape
    parts = asked_refs[0].shape[-2]
    me = lax.axis_index("shard")
    inner = me % INNER
    outer = me // INNER
    tri = before(128)
    count = None
    picked = None
    for part in range(parts):
        if asked_refs[0].ndim == 3:
            block = asked_refs[0][:, part, :]
        else:
            block = jnp.concatenate([r[part : part + 1, :] for r in asked_refs], axis=0)
        owner = block // blk
        valid = owner // INNER == outer
        ones = valid.astype(f32)
        rank = jnp.dot(ones.astype(bf16), tri, preferred_element_type=f32)
        total = jnp.sum(ones, axis=1, keepdims=True)
        if count is not None:
            rank = rank + count
            total = total + count
        count = total
        row = ((owner % INNER) ^ inner) * blk + (block - owner * blk)
        place = jnp.where(valid, rank.astype(i32), -1)[:, None, :]
        value = (row + 1).astype(f32)[:, None, :]
        shape = (place.shape[0], room, 128)
        hit = jnp.broadcast_to(place, shape) == iota(shape, 1)
        here = jnp.where(hit, jnp.broadcast_to(value, shape), 0.0)
        picked = here if picked is None else picked + here
    ids = jnp.sum(picked, axis=2, keepdims=True).astype(i32) - 1
    askers = ids.shape[0]
    shape = (askers, room, blk)
    rows = None
    for j in range(INNER):
        hot = mask(jnp.broadcast_to(ids - j * blk, shape) == iota(shape, 2)).reshape(askers * room, blk)
        term = jnp.dot(hot, table_refs[j][...], preferred_element_type=f32)
        rows = term if rows is None else rows + term
    rows = rows.astype(bf16)
    if out_refs[0].ndim == 3:
        out_refs[0][...] = rows.reshape(askers, room, lane)
    else:
        for k, out_ref in enumerate(out_refs):
            out_ref[...] = rows[k * room : (k + 1) * room]


def state_kernel(z_ref, n_ref, zt_ref, nt_ref):
    half = zt_ref.shape[0]
    rep = lax.axis_index("rep")
    zt = z_ref[...].T
    nt = n_ref[...].T
    zt_ref[...] = jnp.where(rep == 0, zt[:half], zt[half:])
    nt_ref[...] = jnp.where(rep == 0, nt[:half], nt[half:])


def worker_kernel(
    shards, cap, answers, order_ref, take_ref, put_ref, code_ref, labels_ref, tile_ref, *refs
):
    answer_refs = refs[:answers]
    margin_ref, out_ref, w_ref, sum_ref, grad_ref = refs[answers:]
    tiles, lane, _ = tile_ref.shape
    groups = labels_ref.shape[0]
    each = tiles // groups
    answer = [r[...].reshape(-1, lane) for r in answer_refs]
    answer = answer[0] if answers == 1 else jnp.concatenate(answer, axis=0)
    w_ref[...] = jnp.dot(take_ref[...], answer, preferred_element_type=f32)
    for g in range(groups):
        def add(j, acc):
            p = g * each + j
            return acc + tile_ref[order_ref[0, p]].astype(f32) * w_ref[pl.ds(p, 1), :]

        sum_ref[g] = lax.fori_loop(0, each, add, jnp.zeros((lane, lane), f32), unroll=8)
    margins = jnp.concatenate([jnp.sum(sum_ref[g], axis=1).reshape(1, lane) for g in range(groups)], axis=0)
    margin_ref[...] = margins
    resid = (jax.nn.sigmoid(margins) - labels_ref[...].astype(f32)).astype(bf16)
    for g in range(groups):
        row = resid[g : g + 1]
        for j in range(0, each, 2):
            p = g * each + j
            pair = jnp.concatenate([tile_ref[order_ref[0, p]], tile_ref[order_ref[0, p + 1]]], axis=1)
            both = jnp.dot(row, pair, preferred_element_type=f32)
            grad_ref[p : p + 1, :] = both[:, :lane]
            grad_ref[p + 1 : p + 2, :] = both[:, lane:]
    grads = grad_ref[...]
    half = lane // 2
    left = iota((tiles, lane), 1) < half
    code = code_ref[...].astype(f32)
    put = put_ref[...]
    for rep in range(2):
        side = grads if rep == 0 else jnp.concatenate([grads[:, half:], grads[:, :half]], axis=1)
        side = jnp.where(left, side, code).astype(bf16)
        sent = jnp.dot(put, side, preferred_element_type=f32).astype(bf16)
        out_ref[rep * shards : (rep + 1) * shards] = sent.reshape(shards, cap, lane)


def update_kernel(incoming_ref, zt_ref, nt_ref, z_out, n_out, w_out):
    sources, cap, lane = incoming_ref.shape
    half, blk = zt_ref.shape
    rows = sources * cap
    incoming = incoming_ref[...].reshape(rows, lane)
    low = incoming[:, half : half + 1].astype(f32)
    high = incoming[:, half + 1 : half + 2].astype(f32)
    ids = (low + high * 256.0).astype(i32) - 1
    hot = mask(jnp.broadcast_to(ids, (rows, blk)) == iota((rows, blk), 1))
    total = lax.dot_general(incoming, hot, (((0,), (0,)), ((), ())), preferred_element_type=f32)[:half]
    z_state = zt_ref[...]
    n_state = nt_ref[...]
    w_old = shrink(z_state, n_state)
    new_n = n_state + total * total
    sigma = (jnp.sqrt(new_n) - jnp.sqrt(n_state)) / rate_alpha
    new_z = z_state + total - sigma * w_old
    z_out[...] = new_z
    n_out[...] = new_n
    w_out[...] = shrink(new_z, new_n)


def call(kernel, out, specs, scratch=(), limit=16 << 20, flops=0):
    return pl.pallas_call(
        kernel,
        out_shape=out,
        in_specs=specs,
        out_specs=jax.tree.map(lambda _: VMEM, out),
        scratch_shapes=list(scratch),
        compiler_params=pltpu.CompilerParams(vmem_limit_bytes=limit),
        cost_estimate=pl.CostEstimate(flops=flops, bytes_accessed=0, transcendentals=0),
    )


def crossed(x, by):
    size = lax.axis_size("shard")
    return lax.ppermute(x, "shard", [(i, i ^ by) for i in range(size)])


def body(z_state, n_state, tile_values, tile_block, tile_group, labels):
    blk, lane = z_state.shape
    tiles = tile_block.shape[0]
    groups = labels.shape[0]
    shards = lax.axis_size("shard")
    reps = lax.axis_size("rep")
    half = lane // reps
    outers = shards // INNER
    need = max(4, (tiles + shards - 2) // (shards - 1))
    cap = (need + 7) // 8 * 8
    room = (min(INNER * need, tiles) + 15) // 16 * 16
    relative = outers <= 4
    shape = jax.ShapeDtypeStruct

    ids = tile_block.reshape(tiles // 128, 128)
    pull = call(
        pull_kernel,
        shape((blk, lane), bf16),
        [HBM] * 2,
        [pltpu.VMEM((blk, lane), f32)] * 2 + [pltpu.SemaphoreType.DMA((2,))],
        limit=(64 << 20) - 5 * blk * lane // 2,
    )(z_state, n_state)
    if relative:
        asked = [crossed(ids, INNER * k) for k in range(1, outers)]
    else:
        columns = [[b * INNER + a for b in range(outers)] for a in range(INNER)]
        swap = functools.partial(
            lax.all_to_all, axis_name="shard", split_axis=0, concat_axis=0, tiled=True, axis_index_groups=columns
        )
        asked = [swap(jnp.broadcast_to(ids[None], (outers,) + ids.shape))]
    table = [pull] + [crossed(pull, j) for j in range(1, INNER)]

    order, take, put, code = call(
        functools.partial(route_kernel, shards, groups, cap, room, relative, blk),
        (
            shape((1, tiles), i32),
            shape((tiles, outers * room), bf16),
            shape((shards * cap, tiles), bf16),
            shape((tiles, lane), bf16),
        ),
        [VMEM, VMEM],
        flops=8 * 10**9,
    )(tile_block.reshape(1, tiles), tile_group.reshape(1, tiles))
    zt, nt = call(state_kernel, (shape((half, blk), f32),) * 2, [VMEM] * 2)(z_state, n_state)

    def answered(asked, out):
        return call(
            functools.partial(answer_kernel, len(asked), room), out, [VMEM] * (len(asked) + INNER)
        )(*asked, *table)

    if relative:
        replies = answered(asked, (shape((room, lane), bf16),) * (outers - 1))
        answers = [crossed(reply, INNER * (k + 1)) for k, reply in enumerate(replies)]
        answers = list(answered([ids], (shape((room, lane), bf16),))) + answers
    else:
        answers = [swap(answered(asked, shape((outers, room, lane), bf16)))]
    margins, outgoing = call(
        functools.partial(worker_kernel, shards, cap, len(answers)),
        (shape((groups, lane), f32), shape((reps * shards, cap, lane), bf16)),
        [SMEM] + [VMEM] * (5 + len(answers)),
        [pltpu.VMEM((tiles, lane), f32), pltpu.VMEM((groups, lane, lane), f32), pltpu.VMEM((tiles, lane), f32)],
    )(order, take, put, code, labels, tile_values, *answers)
    incoming = lax.all_to_all(outgoing, ("rep", "shard"), split_axis=0, concat_axis=0, tiled=True)
    outs = call(update_kernel, (shape((half, blk), f32),) * 3, [VMEM] * 3)(incoming, zt, nt)
    return (margins,) + tuple(o.T for o in outs)


def solution(mesh):
    placed = (
        P("shard", None),
        P("shard", None),
        P(("rep", "shard"), None, None),
        P(("rep", "shard")),
        P(("rep", "shard")),
        P(("rep", "shard"), None),
    )
    return jax.shard_map(
        body,
        mesh=mesh,
        in_specs=placed,
        out_specs=(
            P(("rep", "shard"), None),
            P("shard", "rep"),
            P("shard", "rep"),
            P("shard", "rep"),
        ),
        check_vma=False,
    )
```

```python
import functools

import jax
import jax.numpy as jnp
from jax import lax
from jax.experimental import pallas as pl
from jax.experimental.pallas import tpu as pltpu
from jax.sharding import PartitionSpec as P

rate_alpha = 0.5
rate_beta = 1.0
lasso_weight = 0.5
ridge_weight = 1.0

f32, bf16, i32 = jnp.float32, jnp.bfloat16, jnp.int32
VMEM = pl.BlockSpec(memory_space=pltpu.VMEM)
SMEM = pl.BlockSpec(memory_space=pltpu.SMEM)


def shrink(z_acc, n_acc):
    soft = z_acc - jnp.clip(z_acc, -lasso_weight, lasso_weight)
    return -soft / ((rate_beta + jnp.sqrt(n_acc)) / rate_alpha + ridge_weight)


def iota(shape, dim):
    return lax.broadcasted_iota(i32, shape, dim)


def mask(hit):
    return hit.astype(f32).astype(bf16)


def before(size):
    return mask(iota((size, size), 0) < iota((size, size), 1))


def slot_ids(asked, cap, first, blk):
    tri = before(128)
    count = None
    picked = None
    for part in range(asked.shape[1]):
        local = asked[:, part, :] - first
        valid = (local >= 0) & (local < blk)
        ones = valid.astype(f32)
        rank = jnp.dot(ones.astype(bf16), tri, preferred_element_type=f32)
        total = jnp.sum(ones, axis=1, keepdims=True)
        if count is not None:
            rank = rank + count
            total = total + count
        count = total
        place = jnp.where(valid, rank.astype(i32), -1)[:, None, :]
        value = (local + 1).astype(f32)[:, None, :]
        shape = (place.shape[0], cap, 128)
        hit = jnp.broadcast_to(place, shape) == iota(shape, 1)
        here = jnp.where(hit, jnp.broadcast_to(value, shape), 0.0)
        picked = here if picked is None else picked + here
    return jnp.sum(picked, axis=2, keepdims=True).astype(i32) - 1


def one_hot_rows(ids, blk):
    rows, cap, _ = ids.shape
    shape = (rows, cap, blk)
    return mask(jnp.broadcast_to(ids, shape) == iota(shape, 2)).reshape(rows * cap, blk)


def prepare_kernel(
    shards, groups, cap, lines, block_ref, group_ref, z_ref, n_ref, pull_ref, order_ref, take_ref, put_ref, zt_ref, nt_ref
):
    blk, _ = z_ref.shape
    half = zt_ref.shape[0]
    tiles = block_ref.shape[1]
    rep = lax.axis_index("rep")
    pull_ref[...] = shrink(z_ref[...], n_ref[...]).astype(bf16)
    zt = z_ref[...].T
    nt = n_ref[...].T
    zt_ref[...] = jnp.where(rep == 0, zt[:half], zt[half:])
    nt_ref[...] = jnp.where(rep == 0, nt[:half], nt[half:])
    tri = before(tiles)
    owner = block_ref[...] // blk
    group = group_ref[...]

    def rank_in(key, count):
        same = jnp.broadcast_to(key, (count, tiles)) == iota((count, tiles), 0)
        rank = jnp.dot(mask(same), tri, preferred_element_type=f32)
        return jnp.sum(jnp.where(same, rank, 0.0), axis=0, keepdims=True)

    rank = rank_in(owner, shards)
    place = (group * (tiles // groups)).astype(f32) + rank_in(group, groups)
    move = (jnp.broadcast_to(place.astype(i32), (tiles, tiles)) == iota((tiles, tiles), 0)).astype(f32)
    slot = owner.astype(f32) * cap + rank
    column = jnp.sum(move * slot, axis=1, keepdims=True).astype(i32)
    take_ref[...] = mask(jnp.broadcast_to(column, (tiles, shards * cap)) == iota((tiles, shards * cap), 1))
    row = iota((8, tiles), 0)
    facts = jnp.where(
        row == 0,
        jnp.broadcast_to(owner.astype(f32), (8, tiles)),
        jnp.where(row == 1, jnp.broadcast_to(rank, (8, tiles)), iota((8, tiles), 1).astype(f32)),
    )
    facts = lax.dot_general(
        facts.astype(bf16), move.astype(bf16), (((1,), (1,)), ((), ())), preferred_element_type=f32
    )
    order_ref[...] = facts[2:3].astype(i32)
    owner = facts[0:1].astype(i32)
    rank = facts[1:2].astype(i32)
    at = iota((shards * lines, tiles), 0)
    left = jnp.where(rank < lines, owner * lines + rank, -1)
    right = jnp.where(rank >= lines, owner * lines + rank - lines, -1)
    put_ref[:, :tiles] = mask(jnp.broadcast_to(left, at.shape) == at)
    put_ref[:, tiles:] = mask(jnp.broadcast_to(right, at.shape) == at)


def answer_kernel(shards, cap, asked_ref, pull_ref, answer_ref):
    blk, lane = pull_ref.shape
    me = lax.axis_index("shard")
    rep = lax.axis_index("rep")
    asked = asked_ref[pl.ds(rep * shards, shards)]
    hot = one_hot_rows(slot_ids(asked, cap, me * blk, blk), blk)
    rows = jnp.dot(hot, pull_ref[...], preferred_element_type=f32)
    answer_ref[...] = rows.astype(bf16).reshape(shards, cap, lane)


def hot_kernel(blk, lines, after_ref, asked_ref, hot_ref):
    me = lax.axis_index("shard")
    ids = slot_ids(asked_ref[...], 2 * lines, me * blk, blk)
    hot_ref[0] = one_hot_rows(ids[:, :lines], blk)
    hot_ref[1] = one_hot_rows(ids[:, lines:], blk)


def worker_kernel(
    shards, cap, order_ref, answer_ref, take_ref, put_ref, labels_ref, tile_ref, margin_ref, out_ref, w_ref, sum_ref, grad_ref
):
    tiles, lane, _ = tile_ref.shape
    groups = labels_ref.shape[0]
    each = tiles // groups
    w_ref[...] = jnp.dot(take_ref[...], answer_ref[...].reshape(shards * cap, lane), preferred_element_type=f32)
    for g in range(groups):
        def add(j, acc):
            p = g * each + j
            return acc + tile_ref[order_ref[0, p]].astype(f32) * w_ref[pl.ds(p, 1), :]

        sum_ref[g] = lax.fori_loop(0, each, add, jnp.zeros((lane, lane), f32), unroll=8)
    margins = jnp.concatenate([jnp.sum(sum_ref[g], axis=1).reshape(1, lane) for g in range(groups)], axis=0)
    margin_ref[...] = margins
    resid = (jax.nn.sigmoid(margins) - labels_ref[...].astype(f32)).astype(bf16)
    for g in range(groups):
        row = resid[g : g + 1]
        wide = jnp.broadcast_to(row.astype(f32), (lane, lane)).T
        for j in range(0, each, 4):
            p = g * each + j
            pair = jnp.concatenate([tile_ref[order_ref[0, p]], tile_ref[order_ref[0, p + 1]]], axis=1)
            both = jnp.dot(row, pair, preferred_element_type=f32)
            grad_ref[p : p + 1, :] = both[:, :lane]
            grad_ref[p + 1 : p + 2, :] = both[:, lane:]
            for q in (p + 2, p + 3):
                grad_ref[q : q + 1, :] = jnp.sum(tile_ref[order_ref[0, q]].astype(f32) * wide, axis=0, keepdims=True)
    grads = grad_ref[...]
    half = lane // 2
    swapped = jnp.concatenate([grads[:, half:], grads[:, :half]], axis=1)
    left = iota((tiles, lane), 1) < half
    put = put_ref[...]
    for rep in range(2):
        first, second = (grads, swapped) if rep == 0 else (swapped, grads)
        sides = jnp.concatenate([jnp.where(left, first, 0.0), jnp.where(left, 0.0, second)], axis=0)
        sent = jnp.dot(put, sides.astype(bf16), preferred_element_type=f32).astype(bf16)
        out_ref[rep * shards : (rep + 1) * shards] = sent.reshape(shards, -1, lane)


def update_kernel(incoming_ref, hot_ref, zt_ref, nt_ref, z_out, n_out, w_out):
    sources, lines, lane = incoming_ref.shape
    half = lane // 2
    incoming = incoming_ref[...].reshape(sources * lines, lane)
    over_rows = (((0,), (0,)), ((), ()))
    left = lax.dot_general(incoming, hot_ref[0], over_rows, preferred_element_type=f32)
    right = lax.dot_general(incoming, hot_ref[1], over_rows, preferred_element_type=f32)
    total = left[:half] + right[half:]
    z_state = zt_ref[...]
    n_state = nt_ref[...]
    w_old = shrink(z_state, n_state)
    new_n = n_state + total * total
    sigma = (jnp.sqrt(new_n) - jnp.sqrt(n_state)) / rate_alpha
    new_z = z_state + total - sigma * w_old
    z_out[...] = new_z
    n_out[...] = new_n
    w_out[...] = shrink(new_z, new_n)


def call(kernel, out, specs, scratch=(), limit=16 << 20, flops=0):
    return pl.pallas_call(
        kernel,
        out_shape=out,
        in_specs=specs,
        out_specs=jax.tree.map(lambda _: VMEM, out),
        scratch_shapes=list(scratch),
        compiler_params=pltpu.CompilerParams(vmem_limit_bytes=limit),
        cost_estimate=pl.CostEstimate(flops=flops, bytes_accessed=0, transcendentals=0),
    )


def body(z_state, n_state, tile_values, tile_block, tile_group, labels):
    blk, lane = z_state.shape
    tiles = tile_block.shape[0]
    groups = labels.shape[0]
    shards = lax.axis_size("shard")
    reps = lax.axis_size("rep")
    half = lane // reps
    need = max(4, (tiles + shards - 2) // (shards - 1))
    cap = (need + 7) // 8 * 8
    lines = 8 if need <= 16 else (need + 31) // 32 * 16
    slots = shards * cap
    axes = ("rep", "shard")
    shape = jax.ShapeDtypeStruct

    raw = jnp.broadcast_to(tile_block.reshape(1, tiles // 128, 128), (reps * shards, tiles // 128, 128))
    asked = lax.all_to_all(raw, axes, split_axis=0, concat_axis=0, tiled=True)
    pull, order, take, put, zt, nt = call(
        functools.partial(prepare_kernel, shards, groups, cap, lines),
        (
            shape((blk, lane), bf16),
            shape((1, tiles), i32),
            shape((tiles, slots), bf16),
            shape((shards * lines, 2 * tiles), bf16),
            shape((half, blk), f32),
            shape((half, blk), f32),
        ),
        [VMEM] * 4,
        flops=4 * 10**9,
    )(tile_block.reshape(1, tiles), tile_group.reshape(1, tiles), z_state, n_state)
    answer = call(
        functools.partial(answer_kernel, shards, cap),
        shape((shards, cap, lane), bf16),
        [VMEM] * 2,
        flops=8 * 10**9,
    )(asked, pull)
    answer = lax.all_to_all(answer, "shard", split_axis=0, concat_axis=0, tiled=True)
    margins, outgoing = call(
        functools.partial(worker_kernel, shards, cap),
        (shape((groups, lane), f32), shape((reps * shards, lines, lane), bf16)),
        [SMEM] + [VMEM] * 5,
        [pltpu.VMEM((tiles, lane), f32), pltpu.VMEM((groups, lane, lane), f32), pltpu.VMEM((tiles, lane), f32)],
    )(order, answer, take, put, labels, tile_values)
    incoming = lax.all_to_all(outgoing, axes, split_axis=0, concat_axis=0, tiled=True)
    hot = call(
        functools.partial(hot_kernel, blk, lines), shape((2, reps * shards * lines, blk), bf16), [VMEM] * 2, flops=4 * 10**9
    )(margins, asked)
    outs = call(update_kernel, (shape((half, blk), f32),) * 3, [VMEM] * 4)(incoming, hot, zt, nt)
    return (margins,) + tuple(o.T for o in outs)


def solution(mesh):
    placed = (
        P("shard", None),
        P("shard", None),
        P(("rep", "shard"), None, None),
        P(("rep", "shard")),
        P(("rep", "shard")),
        P(("rep", "shard"), None),
    )
    return jax.shard_map(
        body,
        mesh=mesh,
        in_specs=placed,
        out_specs=(
            P(("rep", "shard"), None),
            P("shard", "rep"),
            P("shard", "rep"),
            P("shard", "rep"),
        ),
        check_vma=False,
    )
```

```python
import functools

import jax
import jax.numpy as jnp
from jax import lax
from jax.experimental import pallas as pl
from jax.experimental.pallas import tpu as pltpu
from jax.sharding import PartitionSpec as P

rate_alpha = 0.5
rate_beta = 1.0
lasso_weight = 0.5
ridge_weight = 1.0

f32, bf16, i32 = jnp.float32, jnp.bfloat16, jnp.int32
VMEM = pl.BlockSpec(memory_space=pltpu.VMEM)
SMEM = pl.BlockSpec(memory_space=pltpu.SMEM)
HBM = pl.BlockSpec(memory_space=pltpu.HBM)


def shrink(z_acc, n_acc):
    soft = z_acc - jnp.clip(z_acc, -lasso_weight, lasso_weight)
    return -soft / ((rate_beta + jnp.sqrt(n_acc)) / rate_alpha + ridge_weight)


def iota(shape, dim):
    return lax.broadcasted_iota(i32, shape, dim)


def mask(hit):
    return hit.astype(f32).astype(bf16)


def before(size):
    return mask(iota((size, size), 0) < iota((size, size), 1))


def asked_slots(asked, first, blk):
    tri = before(128)
    count = 0.0
    ranks = []
    locals_ = []
    for part in range(asked.shape[1]):
        local = asked[:, part, :] - first
        valid = (local >= 0) & (local < blk)
        ones = valid.astype(f32)
        rank = jnp.dot(ones.astype(bf16), tri, preferred_element_type=f32) + count
        count = count + jnp.sum(ones, axis=1, keepdims=True)
        ranks.append(jnp.where(valid, rank, -1.0))
        locals_.append(jnp.where(valid, local, 0))
    return jnp.concatenate(ranks, axis=1), jnp.concatenate(locals_, axis=1)


def slot_rows(rank, local, lines, *firsts):
    workers, tiles = rank.shape
    rows = workers * lines
    row = iota((rows, workers), 0)
    worker = iota((rows, workers), 1) * lines
    spread = mask((row >= worker) & (row < worker + lines))
    line = (iota((rows, tiles), 0) % lines).astype(f32)
    number = local + 1
    high = number // 256
    low = number - high * 256
    each_rank = jnp.dot(spread, rank.astype(bf16), preferred_element_type=f32)
    each_high = jnp.dot(spread, high.astype(f32).astype(bf16), preferred_element_type=f32)
    each_low = jnp.dot(spread, low.astype(f32).astype(bf16), preferred_element_type=f32)
    each = each_high * 256.0 + each_low
    columns = []
    for first in firsts:
        picked = jnp.where(each_rank - first == line, each, 0.0)
        columns.append(jnp.sum(picked, axis=1, keepdims=True).astype(i32) - 1)
    return columns


def one_hot(column, blk):
    shape = (column.shape[0], blk)
    return mask(jnp.broadcast_to(column, shape) == iota(shape, 1))


def prepare_kernel(
    shards, groups, lines, block_hbm, group_hbm, z_hbm, n_hbm, pull_ref, order_ref, take_ref, put_ref, zt_ref, nt_ref,
    block_ref, group_ref, z_ref, n_ref, sem
):
    copies = [
        pltpu.make_async_copy(source, target, sem.at[i])
        for i, (source, target) in enumerate(
            [(block_hbm, block_ref), (group_hbm, group_ref), (z_hbm, z_ref), (n_hbm, n_ref)]
        )
    ]
    for copy in copies:
        copy.start()
    copies[0].wait()
    copies[1].wait()
    blk, _ = z_ref.shape
    half = zt_ref.shape[0]
    parts = block_ref.shape[0]
    tiles = parts * 128
    rep = lax.axis_index("rep")
    tri = before(tiles)
    owner = jnp.concatenate([block_ref[i : i + 1] for i in range(parts)], axis=1) // blk
    group = jnp.concatenate([group_ref[i : i + 1] for i in range(parts)], axis=1)

    def rank_in(key, count):
        same = jnp.broadcast_to(key, (count, tiles)) == iota((count, tiles), 0)
        rank = jnp.dot(mask(same), tri, preferred_element_type=f32)
        return jnp.sum(jnp.where(same, rank, 0.0), axis=0, keepdims=True)

    rank = rank_in(owner, shards)
    place = (group * (tiles // groups)).astype(f32) + rank_in(group, groups)
    move = (jnp.broadcast_to(place.astype(i32), (tiles, tiles)) == iota((tiles, tiles), 0)).astype(f32)
    late = rank >= lines
    slot = owner.astype(f32) * lines + rank + jnp.where(late, (shards - 1) * lines * 1.0, 0.0)
    column = jnp.sum(move * slot, axis=1, keepdims=True).astype(i32)
    take_ref[...] = mask(jnp.broadcast_to(column, take_ref.shape) == iota(take_ref.shape, 1))
    row = iota((8, tiles), 0)
    facts = jnp.where(
        row == 0,
        jnp.broadcast_to(owner.astype(f32), (8, tiles)),
        jnp.where(row == 1, jnp.broadcast_to(rank, (8, tiles)), iota((8, tiles), 1).astype(f32)),
    )
    facts = lax.dot_general(
        facts.astype(bf16), move.astype(bf16), (((1,), (1,)), ((), ())), preferred_element_type=f32
    )
    order_ref[...] = facts[2:3].astype(i32)
    owner = facts[0:1].astype(i32)
    rank = facts[1:2].astype(i32)
    at = iota((shards * lines, tiles), 0)
    left = jnp.where(rank < lines, owner * lines + rank, -1)
    right = jnp.where(rank >= lines, owner * lines + rank - lines, -1)
    put_ref[:, :tiles] = mask(jnp.broadcast_to(left, at.shape) == at)
    put_ref[:, tiles:] = mask(jnp.broadcast_to(right, at.shape) == at)
    copies[2].wait()
    copies[3].wait()
    pull_ref[...] = shrink(z_ref[...], n_ref[...]).astype(bf16)
    zt = z_ref[...].T
    nt = n_ref[...].T
    zt_ref[...] = jnp.where(rep == 0, zt[:half], zt[half:])
    nt_ref[...] = jnp.where(rep == 0, nt[:half], nt[half:])


def answer_kernel(lines, asked_ref, pull_ref, answer_ref):
    blk, lane = pull_ref.shape
    me = lax.axis_index("shard")
    rep = lax.axis_index("rep")
    rank, local = asked_slots(asked_ref[...], me * blk, blk)
    (column,) = slot_rows(rank, local, lines, (rep * lines).astype(f32))
    answer_ref[...] = jnp.dot(one_hot(column, blk), pull_ref[...], preferred_element_type=f32).astype(bf16)


def worker_kernel(
    lines, order_ref, answer_ref, take_ref, put_ref, labels_ref, asked_ref, tile_ref, margin_ref, out_ref, hot_ref,
    w_ref, sum_ref, grad_ref
):
    tiles, lane, _ = tile_ref.shape
    groups = labels_ref.shape[0]
    each = tiles // groups
    w_ref[...] = jnp.dot(take_ref[...], answer_ref[...], preferred_element_type=f32)
    for g in range(groups):
        def add(j, acc):
            p = g * each + j
            return acc + tile_ref[order_ref[0, p]].astype(f32) * w_ref[pl.ds(p, 1), :]

        sum_ref[g] = lax.fori_loop(0, each, add, jnp.zeros((lane, lane), f32), unroll=8)
    margins = jnp.concatenate([jnp.sum(sum_ref[g], axis=1).reshape(1, lane) for g in range(groups)], axis=0)
    margin_ref[...] = margins
    resid = (jax.nn.sigmoid(margins) - labels_ref[...].astype(f32)).astype(bf16)
    rows, blk = hot_ref.shape[1:]
    share = rows // groups
    rank, local = asked_slots(asked_ref[...], lax.axis_index("shard") * blk, blk)
    columns = slot_rows(rank, local, lines, 0.0, float(lines))
    for g in range(groups):
        for side, column in enumerate(columns):
            hot_ref[side, g * share : (g + 1) * share] = one_hot(column[g * share : (g + 1) * share], blk)
        row = resid[g : g + 1]
        for j in range(0, each, 2):
            p = g * each + j
            pair = jnp.concatenate([tile_ref[order_ref[0, p]], tile_ref[order_ref[0, p + 1]]], axis=1)
            both = jnp.dot(row, pair, preferred_element_type=f32)
            grad_ref[p : p + 1, :] = both[:, :lane]
            grad_ref[p + 1 : p + 2, :] = both[:, lane:]
    grads = grad_ref[...]
    half = lane // 2
    swapped = jnp.concatenate([grads[:, half:], grads[:, :half]], axis=1)
    left = iota((tiles, lane), 1) < half
    put = put_ref[...]
    for rep in range(2):
        first, second = (grads, swapped) if rep == 0 else (swapped, grads)
        sides = jnp.concatenate([jnp.where(left, first, 0.0), jnp.where(left, 0.0, second)], axis=0)
        sent = jnp.dot(put, sides.astype(bf16), preferred_element_type=f32).astype(bf16)
        out_ref[rep * sent.shape[0] : (rep + 1) * sent.shape[0]] = sent


def update_kernel(incoming_ref, hot_ref, zt_ref, nt_ref, z_out, n_out, w_out):
    half = zt_ref.shape[0]
    incoming = incoming_ref[...]
    over_rows = (((0,), (0,)), ((), ()))
    left = lax.dot_general(incoming, hot_ref[0], over_rows, preferred_element_type=f32)
    right = lax.dot_general(incoming, hot_ref[1], over_rows, preferred_element_type=f32)
    total = left[:half] + right[half:]
    z_state = zt_ref[...]
    n_state = nt_ref[...]
    w_old = shrink(z_state, n_state)
    new_n = n_state + total * total
    sigma = (jnp.sqrt(new_n) - jnp.sqrt(n_state)) / rate_alpha
    new_z = z_state + total - sigma * w_old
    z_out[...] = new_z
    n_out[...] = new_n
    w_out[...] = shrink(new_z, new_n)


def call(kernel, out, specs, scratch=(), limit=16 << 20, flops=0):
    return pl.pallas_call(
        kernel,
        out_shape=out,
        in_specs=specs,
        out_specs=jax.tree.map(lambda _: VMEM, out),
        scratch_shapes=list(scratch),
        compiler_params=pltpu.CompilerParams(vmem_limit_bytes=limit),
        cost_estimate=pl.CostEstimate(flops=flops, bytes_accessed=0, transcendentals=0),
    )


def body(z_state, n_state, tile_values, tile_block, tile_group, labels):
    blk, lane = z_state.shape
    tiles = tile_block.shape[0]
    groups = labels.shape[0]
    shards = lax.axis_size("shard")
    reps = lax.axis_size("rep")
    half = lane // reps
    need = max(4, (tiles + shards - 2) // (shards - 1))
    lines = (need + 3) // 4 * 2
    devices = reps * shards
    parts = tiles // 128
    shape = jax.ShapeDtypeStruct
    in_hbm = functools.partial(pltpu.with_memory_space_constraint, memory_space=pltpu.HBM)

    def swap(x):
        return lax.all_to_all(x, ("rep", "shard"), split_axis=0, concat_axis=0, tiled=True)

    def swap_rows(x):
        return swap(x.reshape(devices, lines // 2, 2, lane)).reshape(x.shape)

    ids = tile_block.reshape(parts, 128)
    asked = swap(jnp.broadcast_to(ids[None], (devices, parts, 128)))
    pull, order, take, put, zt, nt = call(
        functools.partial(prepare_kernel, shards, groups, lines),
        (
            shape((blk, lane), bf16),
            shape((1, tiles), i32),
            shape((tiles, devices * lines), bf16),
            shape((shards * lines, 2 * tiles), bf16),
            shape((half, blk), f32),
            shape((half, blk), f32),
        ),
        [HBM] * 4,
        [pltpu.VMEM((parts, 128), i32)] * 2 + [pltpu.VMEM((blk, lane), f32)] * 2 + [pltpu.SemaphoreType.DMA((4,))],
        flops=4 * 10**9,
    )(*(in_hbm(x) for x in (ids, tile_group.reshape(parts, 128), z_state, n_state)))
    answer = call(
        functools.partial(answer_kernel, lines),
        shape((devices * lines, lane), bf16),
        [VMEM] * 2,
        flops=8 * 10**9,
    )(asked, pull)
    margins, outgoing, hot = call(
        functools.partial(worker_kernel, lines),
        (
            shape((groups, lane), f32),
            shape((devices * lines, lane), bf16),
            shape((2, devices * lines, blk), bf16),
        ),
        [SMEM] + [VMEM] * 6,
        [pltpu.VMEM((tiles, lane), f32), pltpu.VMEM((groups, lane, lane), f32), pltpu.VMEM((tiles, lane), f32)],
    )(order, swap_rows(answer), take, put, labels, asked, tile_values)
    incoming = swap_rows(outgoing)
    outs = call(update_kernel, (shape((half, blk), f32),) * 3, [VMEM] * 4)(incoming, hot, zt, nt)
    return (margins,) + tuple(o.T for o in outs)


def solution(mesh):
    placed = (
        P("shard", None),
        P("shard", None),
        P(("rep", "shard"), None, None),
        P(("rep", "shard")),
        P(("rep", "shard")),
        P(("rep", "shard"), None),
    )
    return jax.shard_map(
        body,
        mesh=mesh,
        in_specs=placed,
        out_specs=(
            P(("rep", "shard"), None),
            P("shard", "rep"),
            P("shard", "rep"),
            P("shard", "rep"),
        ),
        check_vma=False,
    )
```

```python
import functools

import jax
import jax.numpy as jnp
from jax import lax
from jax.experimental import pallas as pl
from jax.experimental.pallas import tpu as pltpu
from jax.sharding import PartitionSpec as P

rate_alpha = 0.5
rate_beta = 1.0
lasso_weight = 0.5
ridge_weight = 1.0

f32, bf16, i32 = jnp.float32, jnp.bfloat16, jnp.int32
VMEM = pl.BlockSpec(memory_space=pltpu.VMEM)
SMEM = pl.BlockSpec(memory_space=pltpu.SMEM)
HBM = pl.BlockSpec(memory_space=pltpu.HBM)


def shrink(z_acc, n_acc):
    soft = z_acc - jnp.clip(z_acc, -lasso_weight, lasso_weight)
    return -soft / ((rate_beta + jnp.sqrt(n_acc)) / rate_alpha + ridge_weight)


def iota(shape, dim):
    return lax.broadcasted_iota(i32, shape, dim)


def mask(hit):
    return hit.astype(f32).astype(bf16)


def before(size):
    return mask(iota((size, size), 0) < iota((size, size), 1))


def asked_slots(asked, first, blk):
    tri = before(128)
    count = 0.0
    ranks = []
    locals_ = []
    for part in range(asked.shape[1]):
        local = asked[:, part, :] - first
        valid = (local >= 0) & (local < blk)
        ones = valid.astype(f32)
        rank = jnp.dot(ones.astype(bf16), tri, preferred_element_type=f32) + count
        count = count + jnp.sum(ones, axis=1, keepdims=True)
        ranks.append(jnp.where(valid, rank, -1.0))
        locals_.append(jnp.where(valid, local, 0))
    return jnp.concatenate(ranks, axis=1), jnp.concatenate(locals_, axis=1)


def slot_rows(rank, local, lines, *firsts):
    workers, tiles = rank.shape
    rows = workers * lines
    row = iota((rows, workers), 0)
    worker = iota((rows, workers), 1) * lines
    spread = mask((row >= worker) & (row < worker + lines))
    line = (iota((rows, tiles), 0) % lines).astype(f32)
    number = local + 1
    high = number // 256
    low = number - high * 256
    each_rank = jnp.dot(spread, rank.astype(bf16), preferred_element_type=f32)
    each_high = jnp.dot(spread, high.astype(f32).astype(bf16), preferred_element_type=f32)
    each_low = jnp.dot(spread, low.astype(f32).astype(bf16), preferred_element_type=f32)
    each = each_high * 256.0 + each_low
    columns = []
    for first in firsts:
        picked = jnp.where(each_rank - first == line, each, 0.0)
        columns.append(jnp.sum(picked, axis=1, keepdims=True).astype(i32) - 1)
    return columns


def one_hot(column, blk):
    shape = (column.shape[0], 128)
    wide = jnp.broadcast_to(column, shape).astype(jnp.int16)
    one, zero = jnp.ones(shape, bf16), jnp.zeros(shape, bf16)
    parts = [jnp.where(wide == (iota(shape, 1) + at).astype(jnp.int16), one, zero) for at in range(0, blk, 128)]
    return jnp.concatenate(parts, axis=1)


def prepare_kernel(
    shards, groups, lines, block_hbm, group_hbm, z_hbm, n_hbm, pull_ref, order_ref, take_ref, put_ref, zt_ref, nt_ref,
    block_ref, group_ref, z_ref, n_ref, sem
):
    copies = [
        pltpu.make_async_copy(source, target, sem.at[i])
        for i, (source, target) in enumerate(
            [(block_hbm, block_ref), (group_hbm, group_ref), (z_hbm, z_ref), (n_hbm, n_ref)]
        )
    ]
    for copy in copies:
        copy.start()
    copies[0].wait()
    copies[1].wait()
    blk, _ = z_ref.shape
    half = zt_ref.shape[0]
    parts = block_ref.shape[0]
    tiles = parts * 128
    rep = lax.axis_index("rep")
    tri = before(tiles)
    owner = jnp.concatenate([block_ref[i : i + 1] for i in range(parts)], axis=1) // blk
    group = jnp.concatenate([group_ref[i : i + 1] for i in range(parts)], axis=1)

    def rank_in(key, count):
        same = jnp.broadcast_to(key, (count, tiles)) == iota((count, tiles), 0)
        rank = jnp.dot(mask(same), tri, preferred_element_type=f32)
        return jnp.sum(jnp.where(same, rank, 0.0), axis=0, keepdims=True)

    rank = rank_in(owner, shards)
    place = (group * (tiles // groups)).astype(f32) + rank_in(group, groups)
    move = (jnp.broadcast_to(place.astype(i32), (tiles, tiles)) == iota((tiles, tiles), 0)).astype(f32)
    late = rank >= lines
    slot = owner.astype(f32) * lines + rank + jnp.where(late, (shards - 1) * lines * 1.0, 0.0)
    column = jnp.sum(move * slot, axis=1, keepdims=True).astype(i32)
    take_ref[...] = mask(jnp.broadcast_to(column, take_ref.shape) == iota(take_ref.shape, 1))
    row = iota((8, tiles), 0)
    facts = jnp.where(
        row == 0,
        jnp.broadcast_to(owner.astype(f32), (8, tiles)),
        jnp.where(row == 1, jnp.broadcast_to(rank, (8, tiles)), iota((8, tiles), 1).astype(f32)),
    )
    facts = lax.dot_general(
        facts.astype(bf16), move.astype(bf16), (((1,), (1,)), ((), ())), preferred_element_type=f32
    )
    order_ref[...] = facts[2:3].astype(i32)
    owner = facts[0:1].astype(i32)
    rank = facts[1:2].astype(i32)
    at = iota((shards * lines, tiles), 0)
    left = jnp.where(rank < lines, owner * lines + rank, -1)
    right = jnp.where(rank >= lines, owner * lines + rank - lines, -1)
    put_ref[:, :tiles] = mask(jnp.broadcast_to(left, at.shape) == at)
    put_ref[:, tiles:] = mask(jnp.broadcast_to(right, at.shape) == at)
    copies[2].wait()
    copies[3].wait()
    pull_ref[...] = shrink(z_ref[...], n_ref[...]).astype(bf16)
    zt = z_ref[...].T
    nt = n_ref[...].T
    zt_ref[...] = jnp.where(rep == 0, zt[:half], zt[half:])
    nt_ref[...] = jnp.where(rep == 0, nt[:half], nt[half:])


def answer_kernel(lines, asked_ref, pull_ref, answer_ref, hot_ref):
    blk, lane = pull_ref.shape
    me = lax.axis_index("shard")
    rep = lax.axis_index("rep")
    rank, local = asked_slots(asked_ref[...], me * blk, blk)
    (column,) = slot_rows(rank, local, lines, (rep * lines).astype(f32))
    hot = one_hot(column, blk)
    hot_ref[...] = hot
    answer_ref[...] = jnp.dot(hot, pull_ref[...], preferred_element_type=f32).astype(bf16)


def worker_kernel(
    lines, order_vmem, answer_ref, take_ref, put_ref, labels_ref, asked_ref, tile_ref, margin_ref, out_ref, hot_ref,
    w_ref, grad_ref, order_ref, sem
):
    tiles, lane, _ = tile_ref.shape
    groups = labels_ref.shape[0]
    each = tiles // groups
    order_copy = pltpu.make_async_copy(order_vmem, order_ref, sem)
    order_copy.start()
    blk = hot_ref.shape[1]
    rank, local = asked_slots(asked_ref[...], lax.axis_index("shard") * blk, blk)
    other = (1 - lax.axis_index("rep")) * lines
    (column,) = slot_rows(rank, local, lines, other.astype(f32))
    hot_ref[...] = one_hot(column, blk)
    w_ref[...] = jnp.dot(take_ref[...], answer_ref[...], preferred_element_type=f32)
    order_copy.wait()
    resid = None
    for g in range(groups + 1):
        if g < groups:
            total = jnp.zeros((lane, lane), f32)
            for p in range(g * each, (g + 1) * each):
                total = total + tile_ref[order_ref[0, p]].astype(f32) * w_ref[p : p + 1, :]
            margin = jnp.sum(total, axis=1).reshape(1, lane)
            margin_ref[g : g + 1, :] = margin
        if g > 0:
            for p in range((g - 1) * each, g * each, 2):
                pair = jnp.concatenate([tile_ref[order_ref[0, p]], tile_ref[order_ref[0, p + 1]]], axis=1)
                both = jnp.dot(resid, pair, preferred_element_type=f32)
                grad_ref[p : p + 1, :] = both[:, :lane]
                grad_ref[p + 1 : p + 2, :] = both[:, lane:]
        if g < groups:
            resid = (jax.nn.sigmoid(margin) - labels_ref[g : g + 1, :].astype(f32)).astype(bf16)
    grads = grad_ref[...]
    half = lane // 2
    swapped = jnp.concatenate([grads[:, half:], grads[:, :half]], axis=1)
    left = iota((tiles, lane), 1) < half
    put = put_ref[...]
    for rep in range(2):
        first, second = (grads, swapped) if rep == 0 else (swapped, grads)
        sides = jnp.concatenate([jnp.where(left, first, 0.0), jnp.where(left, 0.0, second)], axis=0)
        sent = jnp.dot(put, sides.astype(bf16), preferred_element_type=f32).astype(bf16)
        out_ref[rep * sent.shape[0] : (rep + 1) * sent.shape[0]] = sent


def update_kernel(incoming_ref, mine_ref, other_ref, zt_ref, nt_ref, z_out, n_out, w_out):
    half = zt_ref.shape[0]
    incoming = incoming_ref[...]
    over_rows = (((0,), (0,)), ((), ()))
    mine = lax.dot_general(incoming, mine_ref[...], over_rows, preferred_element_type=f32)
    other = lax.dot_general(incoming, other_ref[...], over_rows, preferred_element_type=f32)
    first = lax.axis_index("rep") == 0
    total = jnp.where(first, mine[:half] + other[half:], mine[half:] + other[:half])
    z_state = zt_ref[...]
    n_state = nt_ref[...]
    w_old = shrink(z_state, n_state)
    new_n = n_state + total * total
    sigma = (jnp.sqrt(new_n) - jnp.sqrt(n_state)) / rate_alpha
    new_z = z_state + total - sigma * w_old
    z_out[...] = new_z
    n_out[...] = new_n
    w_out[...] = shrink(new_z, new_n)


def call(kernel, out, specs, scratch=(), limit=16 << 20, flops=0):
    return pl.pallas_call(
        kernel,
        out_shape=out,
        in_specs=specs,
        out_specs=jax.tree.map(lambda _: VMEM, out),
        scratch_shapes=list(scratch),
        compiler_params=pltpu.CompilerParams(vmem_limit_bytes=limit),
        cost_estimate=pl.CostEstimate(flops=flops, bytes_accessed=0, transcendentals=0),
    )


def body(z_state, n_state, tile_values, tile_block, tile_group, labels):
    blk, lane = z_state.shape
    tiles = tile_block.shape[0]
    groups = labels.shape[0]
    shards = lax.axis_size("shard")
    reps = lax.axis_size("rep")
    half = lane // reps
    need = max(4, (tiles + shards - 2) // (shards - 1))
    lines = (need + 3) // 4 * 2
    devices = reps * shards
    parts = tiles // 128
    shape = jax.ShapeDtypeStruct
    in_hbm = functools.partial(pltpu.with_memory_space_constraint, memory_space=pltpu.HBM)

    def swap(x):
        return lax.all_to_all(x, ("rep", "shard"), split_axis=0, concat_axis=0, tiled=True)

    def swap_rows(x):
        return swap(x.reshape(devices, lines // 2, 2, lane)).reshape(x.shape)

    ids = tile_block.reshape(parts, 128)
    asked = swap(jnp.broadcast_to(ids[None], (devices, parts, 128)))
    pull, order, take, put, zt, nt = call(
        functools.partial(prepare_kernel, shards, groups, lines),
        (
            shape((blk, lane), bf16),
            shape((1, tiles), i32),
            shape((tiles, devices * lines), bf16),
            shape((shards * lines, 2 * tiles), bf16),
            shape((half, blk), f32),
            shape((half, blk), f32),
        ),
        [HBM] * 4,
        [pltpu.VMEM((parts, 128), i32)] * 2 + [pltpu.VMEM((blk, lane), f32)] * 2 + [pltpu.SemaphoreType.DMA((4,))],
        flops=4 * 10**9,
    )(*(in_hbm(x) for x in (ids, tile_group.reshape(parts, 128), z_state, n_state)))
    answer, mine = call(
        functools.partial(answer_kernel, lines),
        (shape((devices * lines, lane), bf16), shape((devices * lines, blk), bf16)),
        [VMEM] * 2,
        flops=8 * 10**9,
    )(asked, pull)
    margins, outgoing, other = call(
        functools.partial(worker_kernel, lines),
        (
            shape((groups, lane), f32),
            shape((devices * lines, lane), bf16),
            shape((devices * lines, blk), bf16),
        ),
        [VMEM] * 7,
        [
            pltpu.VMEM((tiles, lane), f32),
            pltpu.VMEM((tiles, lane), f32),
            pltpu.SMEM((1, tiles), i32),
            pltpu.SemaphoreType.DMA,
        ],
    )(order, swap_rows(answer), take, put, labels, asked, tile_values)
    incoming = swap_rows(outgoing)
    outs = call(update_kernel, (shape((half, blk), f32),) * 3, [VMEM] * 5)(incoming, mine, other, zt, nt)
    return (margins,) + tuple(o.T for o in outs)


def solution(mesh):
    placed = (
        P("shard", None),
        P("shard", None),
        P(("rep", "shard"), None, None),
        P(("rep", "shard")),
        P(("rep", "shard")),
        P(("rep", "shard"), None),
    )
    return jax.shard_map(
        body,
        mesh=mesh,
        in_specs=placed,
        out_specs=(
            P(("rep", "shard"), None),
            P("shard", "rep"),
            P("shard", "rep"),
            P("shard", "rep"),
        ),
        check_vma=False,
    )
```

```python
import functools

import jax
import jax.numpy as jnp
from jax import lax
from jax.experimental import pallas as pl
from jax.experimental.pallas import tpu as pltpu
from jax.sharding import PartitionSpec as P

rate_alpha = 0.5
rate_beta = 1.0
lasso_weight = 0.5
ridge_weight = 1.0

f32, bf16, i32 = jnp.float32, jnp.bfloat16, jnp.int32
VMEM = pl.BlockSpec(memory_space=pltpu.VMEM)
SMEM = pl.BlockSpec(memory_space=pltpu.SMEM)
HBM = pl.BlockSpec(memory_space=pltpu.HBM)


def shrink(z_acc, n_acc):
    soft = z_acc - jnp.clip(z_acc, -lasso_weight, lasso_weight)
    return -soft / ((rate_beta + jnp.sqrt(n_acc)) / rate_alpha + ridge_weight)


def iota(shape, dim):
    return lax.broadcasted_iota(i32, shape, dim)


def mask(hit):
    return hit.astype(f32).astype(bf16)


def before(size):
    return mask(iota((size, size), 0) < iota((size, size), 1))


def asked_slots(asked, first, blk):
    local = jnp.concatenate([asked[:, part, :] for part in range(asked.shape[1])], axis=1) - first
    valid = (local >= 0) & (local < blk)
    rank = jnp.dot(mask(valid), before(local.shape[1]), preferred_element_type=f32)
    return jnp.where(valid, rank, -1.0), jnp.where(valid, local, 0)


def slot_rows(rank, local, lines, *firsts):
    workers, tiles = rank.shape
    rows = workers * lines
    row = iota((rows, workers), 0)
    worker = iota((rows, workers), 1) * lines
    spread = mask((row >= worker) & (row < worker + lines))
    line = (iota((rows, tiles), 0) % lines).astype(f32)
    number = local + 1
    high = number // 256
    low = number - high * 256
    facts = jnp.concatenate([rank, high.astype(f32), low.astype(f32)], axis=1).astype(bf16)
    facts = jnp.dot(spread, facts, preferred_element_type=f32)
    each_rank = facts[:, :tiles]
    each = facts[:, tiles : 2 * tiles] * 256.0 + facts[:, 2 * tiles :]
    columns = []
    for first in firsts:
        picked = jnp.where(each_rank - first == line, each, 0.0)
        columns.append(jnp.sum(picked, axis=1, keepdims=True).astype(i32) - 1)
    return columns


def one_hot(column, blk):
    shape = (column.shape[0], 128)
    wide = jnp.broadcast_to(column, shape).astype(jnp.int16)
    one, zero = jnp.ones(shape, bf16), jnp.zeros(shape, bf16)
    parts = [jnp.where(wide == (iota(shape, 1) + at).astype(jnp.int16), one, zero) for at in range(0, blk, 128)]
    return jnp.concatenate(parts, axis=1)


def prepare_kernel(
    shards, groups, lines, block_hbm, group_hbm, z_hbm, n_hbm, pull_ref, order_ref, take_ref, put_ref, zt_ref, nt_ref,
    wt_ref, rt_ref,    block_ref, group_ref, z_ref, n_ref, sem
):
    copies = [
        pltpu.make_async_copy(source, target, sem.at[i])
        for i, (source, target) in enumerate(
            [(block_hbm, block_ref), (group_hbm, group_ref), (z_hbm, z_ref), (n_hbm, n_ref)]
        )
    ]
    for copy in copies:
        copy.start()
    copies[0].wait()
    copies[1].wait()
    blk, _ = z_ref.shape
    half = zt_ref.shape[0]
    parts = block_ref.shape[0]
    tiles = parts * 128
    rep = lax.axis_index("rep")
    tri = before(tiles)
    owner = jnp.concatenate([block_ref[i : i + 1] for i in range(parts)], axis=1) // blk
    group = jnp.concatenate([group_ref[i : i + 1] for i in range(parts)], axis=1)

    def rank_in(key, count):
        same = jnp.broadcast_to(key, (count, tiles)) == iota((count, tiles), 0)
        rank = jnp.dot(mask(same), tri, preferred_element_type=f32)
        return jnp.sum(jnp.where(same, rank, 0.0), axis=0, keepdims=True)

    rank = rank_in(owner, shards)
    place = (group * (tiles // groups)).astype(f32) + rank_in(group, groups)
    move = (jnp.broadcast_to(place.astype(i32), (tiles, tiles)) == iota((tiles, tiles), 0)).astype(f32)
    late = rank >= lines
    slot = owner.astype(f32) * lines + rank + jnp.where(late, (shards - 1) * lines * 1.0, 0.0)
    column = jnp.sum(move * slot, axis=1, keepdims=True).astype(i32)
    take_ref[...] = mask(jnp.broadcast_to(column, take_ref.shape) == iota(take_ref.shape, 1))
    row = iota((8, tiles), 0)
    facts = jnp.where(
        row == 0,
        jnp.broadcast_to(owner.astype(f32), (8, tiles)),
        jnp.where(row == 1, jnp.broadcast_to(rank, (8, tiles)), iota((8, tiles), 1).astype(f32)),
    )
    facts = lax.dot_general(
        facts.astype(bf16), move.astype(bf16), (((1,), (1,)), ((), ())), preferred_element_type=f32
    )
    order_ref[...] = facts[2:3].astype(i32)
    owner = facts[0:1].astype(i32)
    rank = facts[1:2].astype(i32)
    at = iota((shards * lines, tiles), 0)
    left = jnp.where(rank < lines, owner * lines + rank, -1)
    right = jnp.where(rank >= lines, owner * lines + rank - lines, -1)
    put_ref[:, :tiles] = mask(jnp.broadcast_to(left, at.shape) == at)
    put_ref[:, tiles:] = mask(jnp.broadcast_to(right, at.shape) == at)
    copies[2].wait()
    copies[3].wait()
    pull_ref[...] = shrink(z_ref[...], n_ref[...]).astype(bf16)
    zt = z_ref[...].T
    nt = n_ref[...].T
    zt = jnp.where(rep == 0, zt[:half], zt[half:])
    nt = jnp.where(rep == 0, nt[:half], nt[half:])
    zt_ref[...] = zt
    nt_ref[...] = nt
    wt_ref[...] = shrink(zt, nt)
    rt_ref[...] = jnp.sqrt(nt)


def answer_kernel(lines, asked_ref, pull_ref, answer_ref, hot_ref):
    blk, lane = pull_ref.shape
    me = lax.axis_index("shard")
    rep = lax.axis_index("rep")
    rank, local = asked_slots(asked_ref[...], me * blk, blk)
    (column,) = slot_rows(rank, local, lines, (rep * lines).astype(f32))
    hot = one_hot(column, blk)
    hot_ref[...] = hot
    answer_ref[...] = jnp.dot(hot, pull_ref[...], preferred_element_type=f32).astype(bf16)


def worker_kernel(
    lines, order_vmem, answer_ref, take_ref, put_ref, labels_ref, asked_ref, tile_ref, margin_hbm, out_ref, hot_ref,
    w_ref, grad_ref, margin_ref, order_ref, sem
):
    tiles, lane, _ = tile_ref.shape
    groups = labels_ref.shape[0]
    each = tiles // groups
    order_copy = pltpu.make_async_copy(order_vmem, order_ref, sem.at[0])
    margin_copy = pltpu.make_async_copy(margin_ref, margin_hbm, sem.at[1])
    order_copy.start()
    blk = hot_ref.shape[1]
    rank, local = asked_slots(asked_ref[...], lax.axis_index("shard") * blk, blk)
    other = (1 - lax.axis_index("rep")) * lines
    (column,) = slot_rows(rank, local, lines, other.astype(f32))
    hot_ref[...] = one_hot(column, blk)
    w_ref[...] = jnp.dot(take_ref[...], answer_ref[...], preferred_element_type=f32)
    order_copy.wait()
    resid = None
    for g in range(groups + 1):
        if g < groups:
            total = jnp.zeros((lane, lane), f32)
            for p in range(g * each, (g + 1) * each):
                total = total + tile_ref[order_ref[0, p]].astype(f32) * w_ref[p : p + 1, :]
            margin = jnp.sum(total, axis=1).reshape(1, lane)
            margin_ref[g : g + 1, :] = margin
        if g == groups - 1:
            margin_copy.start()
        if g > 0:
            for p in range((g - 1) * each, g * each, 2):
                pair = jnp.concatenate([tile_ref[order_ref[0, p]], tile_ref[order_ref[0, p + 1]]], axis=1)
                both = jnp.dot(resid, pair, preferred_element_type=f32)
                grad_ref[p : p + 1, :] = both[:, :lane]
                grad_ref[p + 1 : p + 2, :] = both[:, lane:]
        if g < groups:
            resid = (jax.nn.sigmoid(margin) - labels_ref[g : g + 1, :].astype(f32)).astype(bf16)
    grads = grad_ref[...]
    half = lane // 2
    swapped = jnp.concatenate([grads[:, half:], grads[:, :half]], axis=1)
    left = iota((tiles, lane), 1) < half
    put = put_ref[...]
    for rep in range(2):
        first, second = (grads, swapped) if rep == 0 else (swapped, grads)
        sides = jnp.concatenate([jnp.where(left, first, 0.0), jnp.where(left, 0.0, second)], axis=0)
        sent = jnp.dot(put, sides.astype(bf16), preferred_element_type=f32).astype(bf16)
        out_ref[rep * sent.shape[0] : (rep + 1) * sent.shape[0]] = sent
    margin_copy.wait()


def update_kernel(incoming_ref, mine_ref, other_ref, zt_ref, nt_ref, wt_ref, rt_ref, z_out, n_out, w_out):
    half = zt_ref.shape[0]
    incoming = incoming_ref[...]
    over_rows = (((0,), (0,)), ((), ()))
    mine = lax.dot_general(incoming, mine_ref[...], over_rows, preferred_element_type=f32)
    other = lax.dot_general(incoming, other_ref[...], over_rows, preferred_element_type=f32)
    first = lax.axis_index("rep") == 0
    total = jnp.where(first, mine[:half] + other[half:], mine[half:] + other[:half])
    z_state = zt_ref[...]
    n_state = nt_ref[...]
    new_n = n_state + total * total
    sigma = (jnp.sqrt(new_n) - rt_ref[...]) / rate_alpha
    new_z = z_state + total - sigma * wt_ref[...]
    z_out[...] = new_z
    n_out[...] = new_n
    w_out[...] = shrink(new_z, new_n)


def call(kernel, out, specs, scratch=(), limit=16 << 20, flops=0, out_specs=None):
    return pl.pallas_call(
        kernel,
        out_shape=out,
        in_specs=specs,
        out_specs=jax.tree.map(lambda _: VMEM, out) if out_specs is None else out_specs,
        scratch_shapes=list(scratch),
        compiler_params=pltpu.CompilerParams(vmem_limit_bytes=limit),
        cost_estimate=pl.CostEstimate(flops=flops, bytes_accessed=0, transcendentals=0),
    )


def body(z_state, n_state, tile_values, tile_block, tile_group, labels):
    blk, lane = z_state.shape
    tiles = tile_block.shape[0]
    groups = labels.shape[0]
    shards = lax.axis_size("shard")
    reps = lax.axis_size("rep")
    half = lane // reps
    need = max(4, (tiles + shards - 2) // (shards - 1))
    lines = (need + 3) // 4 * 2
    devices = reps * shards
    parts = tiles // 128
    shape = jax.ShapeDtypeStruct
    in_hbm = functools.partial(pltpu.with_memory_space_constraint, memory_space=pltpu.HBM)

    def swap(x):
        return lax.all_to_all(x, ("rep", "shard"), split_axis=0, concat_axis=0, tiled=True)

    def swap_rows(x):
        return swap(x.reshape(devices, lines // 2, 2, lane)).reshape(x.shape)

    ids = tile_block.reshape(parts, 128)
    asked = swap(jnp.broadcast_to(ids[None], (devices, parts, 128)))
    pull, order, take, put, *state = call(
        functools.partial(prepare_kernel, shards, groups, lines),
        (
            shape((blk, lane), bf16),
            shape((1, tiles), i32),
            shape((tiles, devices * lines), bf16),
            shape((shards * lines, 2 * tiles), bf16),
        )
        + (shape((half, blk), f32),) * 4,
        [HBM] * 4,
        [pltpu.VMEM((parts, 128), i32)] * 2 + [pltpu.VMEM((blk, lane), f32)] * 2 + [pltpu.SemaphoreType.DMA((4,))],
        flops=4 * 10**9,
    )(*(in_hbm(x) for x in (ids, tile_group.reshape(parts, 128), z_state, n_state)))
    answer, mine = call(
        functools.partial(answer_kernel, lines),
        (shape((devices * lines, lane), bf16), shape((devices * lines, blk), bf16)),
        [VMEM] * 2,
        flops=8 * 10**9,
    )(asked, pull)
    margins, outgoing, other = call(
        functools.partial(worker_kernel, lines),
        (
            shape((groups, lane), f32),
            shape((devices * lines, lane), bf16),
            shape((devices * lines, blk), bf16),
        ),
        [VMEM] * 7,
        [
            pltpu.VMEM((tiles, lane), f32),
            pltpu.VMEM((tiles, lane), f32),
            pltpu.VMEM((groups, lane), f32),
            pltpu.SMEM((1, tiles), i32),
            pltpu.SemaphoreType.DMA((2,)),
        ],
        out_specs=(HBM, VMEM, VMEM),
    )(order, swap_rows(answer), take, put, labels, asked, tile_values)
    incoming = swap_rows(outgoing)
    outs = call(update_kernel, (shape((half, blk), f32),) * 3, [VMEM] * 7)(incoming, mine, other, *state)
    return (margins,) + tuple(o.T for o in outs)


def solution(mesh):
    placed = (
        P("shard", None),
        P("shard", None),
        P(("rep", "shard"), None, None),
        P(("rep", "shard")),
        P(("rep", "shard")),
        P(("rep", "shard"), None),
    )
    return jax.shard_map(
        body,
        mesh=mesh,
        in_specs=placed,
        out_specs=(
            P(("rep", "shard"), None),
            P("shard", "rep"),
            P("shard", "rep"),
            P("shard", "rep"),
        ),
        check_vma=False,
    )
```

```python
import functools

import jax
import jax.numpy as jnp
from jax import lax
from jax.experimental import pallas as pl
from jax.experimental.pallas import tpu as pltpu
from jax.sharding import PartitionSpec as P

rate_alpha = 0.5
rate_beta = 1.0
lasso_weight = 0.5
ridge_weight = 1.0

f32, bf16, i32 = jnp.float32, jnp.bfloat16, jnp.int32
VMEM = pl.BlockSpec(memory_space=pltpu.VMEM)
SMEM = pl.BlockSpec(memory_space=pltpu.SMEM)
HBM = pl.BlockSpec(memory_space=pltpu.HBM)


def shrink(z_acc, n_acc):
    soft = z_acc - jnp.clip(z_acc, -lasso_weight, lasso_weight)
    return -soft / ((rate_beta + jnp.sqrt(n_acc)) / rate_alpha + ridge_weight)


def iota(shape, dim):
    return lax.broadcasted_iota(i32, shape, dim)


def mask(hit):
    return hit.astype(f32).astype(bf16)


def before(size):
    return mask(iota((size, size), 0) < iota((size, size), 1))


def asked_slots(asked, first, blk):
    local = jnp.concatenate([asked[:, part, :] for part in range(asked.shape[1])], axis=1) - first
    valid = (local >= 0) & (local < blk)
    rank = jnp.dot(mask(valid), before(local.shape[1]), preferred_element_type=f32)
    return jnp.where(valid, rank, -1.0), jnp.where(valid, local, 0)


def slot_rows(rank, local, lines, *firsts):
    workers, tiles = rank.shape
    rows = workers * lines
    row = iota((rows, workers), 0)
    worker = iota((rows, workers), 1) * lines
    spread = mask((row >= worker) & (row < worker + lines))
    line = (iota((rows, tiles), 0) % lines).astype(f32)
    number = local + 1
    high = number // 256
    low = number - high * 256
    facts = jnp.concatenate([rank, high.astype(f32), low.astype(f32)], axis=1).astype(bf16)
    facts = jnp.dot(spread, facts, preferred_element_type=f32)
    each_rank = facts[:, :tiles]
    each = facts[:, tiles : 2 * tiles] * 256.0 + facts[:, 2 * tiles :]
    columns = []
    for first in firsts:
        picked = jnp.where(each_rank - first == line, each, 0.0)
        columns.append(jnp.sum(picked, axis=1, keepdims=True).astype(i32) - 1)
    return columns


def one_hot(column, blk):
    shape = (column.shape[0], 128)
    wide = jnp.broadcast_to(column, shape).astype(jnp.int16)
    one, zero = jnp.ones(shape, bf16), jnp.zeros(shape, bf16)
    parts = [jnp.where(wide == (iota(shape, 1) + at).astype(jnp.int16), one, zero) for at in range(0, blk, 128)]
    return jnp.concatenate(parts, axis=1)


def prepare_kernel(
    shards, groups, lines, block_hbm, group_hbm, z_hbm, n_hbm, pull_ref, order_ref, take_ref, put_ref, zt_ref, nt_ref,
    wt_ref, rt_ref,    block_ref, group_ref, z_ref, n_ref, sem
):
    copies = [
        pltpu.make_async_copy(source, target, sem.at[i])
        for i, (source, target) in enumerate(
            [(block_hbm, block_ref), (group_hbm, group_ref), (z_hbm, z_ref), (n_hbm, n_ref)]
        )
    ]
    for copy in copies:
        copy.start()
    copies[0].wait()
    copies[1].wait()
    blk, _ = z_ref.shape
    half = zt_ref.shape[0]
    parts = block_ref.shape[0]
    tiles = parts * 128
    rep = lax.axis_index("rep")
    tri = before(tiles)
    owner = jnp.concatenate([block_ref[i : i + 1] for i in range(parts)], axis=1) // blk
    group = jnp.concatenate([group_ref[i : i + 1] for i in range(parts)], axis=1)

    def rank_in(key, count):
        same = jnp.broadcast_to(key, (count, tiles)) == iota((count, tiles), 0)
        rank = jnp.dot(mask(same), tri, preferred_element_type=f32)
        return jnp.sum(jnp.where(same, rank, 0.0), axis=0, keepdims=True)

    rank = rank_in(owner, shards)
    place = (group * (tiles // groups)).astype(f32) + rank_in(group, groups)
    move = (jnp.broadcast_to(place.astype(i32), (tiles, tiles)) == iota((tiles, tiles), 0)).astype(f32)
    late = rank >= lines
    slot = owner.astype(f32) * lines + rank + jnp.where(late, (shards - 1) * lines * 1.0, 0.0)
    column = jnp.sum(move * slot, axis=1, keepdims=True).astype(i32)
    take_ref[...] = mask(jnp.broadcast_to(column, take_ref.shape) == iota(take_ref.shape, 1))
    row = iota((8, tiles), 0)
    facts = jnp.where(
        row == 0,
        jnp.broadcast_to(owner.astype(f32), (8, tiles)),
        jnp.where(row == 1, jnp.broadcast_to(rank, (8, tiles)), iota((8, tiles), 1).astype(f32)),
    )
    facts = lax.dot_general(
        facts.astype(bf16), move.astype(bf16), (((1,), (1,)), ((), ())), preferred_element_type=f32
    )
    order_ref[...] = facts[2:3].astype(i32)
    owner = facts[0:1].astype(i32)
    rank = facts[1:2].astype(i32)
    at = iota((shards * lines, tiles), 0)
    left = jnp.where(rank < lines, owner * lines + rank, -1)
    right = jnp.where(rank >= lines, owner * lines + rank - lines, -1)
    put_ref[:, :tiles] = mask(jnp.broadcast_to(left, at.shape) == at)
    put_ref[:, tiles:] = mask(jnp.broadcast_to(right, at.shape) == at)
    copies[2].wait()
    copies[3].wait()
    pull_ref[...] = shrink(z_ref[...], n_ref[...]).astype(bf16)
    zt = z_ref[...].T
    nt = n_ref[...].T
    zt = jnp.where(rep == 0, zt[:half], zt[half:])
    nt = jnp.where(rep == 0, nt[:half], nt[half:])
    zt_ref[...] = zt
    nt_ref[...] = nt
    wt_ref[...] = shrink(zt, nt)
    rt_ref[...] = jnp.sqrt(nt)


def answer_kernel(lines, asked_ref, pull_ref, answer_ref, hot_ref):
    blk, lane = pull_ref.shape
    me = lax.axis_index("shard")
    rep = lax.axis_index("rep")
    rank, local = asked_slots(asked_ref[...], me * blk, blk)
    (column,) = slot_rows(rank, local, lines, (rep * lines).astype(f32))
    hot = one_hot(column, blk)
    hot_ref[...] = hot
    answer_ref[...] = jnp.dot(hot, pull_ref[...], preferred_element_type=f32).astype(bf16)


def worker_kernel(
    lines, order_vmem, answer_ref, take_ref, put_ref, labels_ref, asked_ref, tile_ref, margin_hbm, out_ref, hot_ref,
    w_ref, grad_ref, margin_ref, order_ref, sem
):
    tiles, lane, _ = tile_ref.shape
    groups = labels_ref.shape[0]
    each = tiles // groups
    order_copy = pltpu.make_async_copy(order_vmem, order_ref, sem.at[0])
    margin_copy = pltpu.make_async_copy(margin_ref, margin_hbm, sem.at[1])
    order_copy.start()
    blk = hot_ref.shape[1]
    rank, local = asked_slots(asked_ref[...], lax.axis_index("shard") * blk, blk)
    other = (1 - lax.axis_index("rep")) * lines
    (column,) = slot_rows(rank, local, lines, other.astype(f32))
    hot_ref[...] = one_hot(column, blk)
    w_ref[...] = jnp.dot(take_ref[...], answer_ref[...], preferred_element_type=f32)
    order_copy.wait()
    resid = []
    for g in range(groups + 1):
        if g < groups:
            total = jnp.zeros((lane, lane), f32)
            for p in range(g * each, (g + 1) * each):
                total = total + tile_ref[order_ref[0, p]].astype(f32) * w_ref[p : p + 1, :]
            margin = jnp.sum(total, axis=1).reshape(1, lane)
            margin_ref[g : g + 1, :] = margin
            resid.append((jax.nn.sigmoid(margin) - labels_ref[g : g + 1, :].astype(f32)).astype(bf16))
        if g == groups - 1:
            margin_copy.start()
        if g > 0:
            for p in range((g - 1) * each, g * each, 2):
                pair = jnp.concatenate([tile_ref[order_ref[0, p]], tile_ref[order_ref[0, p + 1]]], axis=1)
                both = jnp.dot(resid[g - 1], pair, preferred_element_type=f32)
                grad_ref[p : p + 1, :] = both[:, :lane]
                grad_ref[p + 1 : p + 2, :] = both[:, lane:]
    grads = grad_ref[...]
    half = lane // 2
    swapped = jnp.concatenate([grads[:, half:], grads[:, :half]], axis=1)
    left = iota((tiles, lane), 1) < half
    put = put_ref[...]
    for rep in range(2):
        first, second = (grads, swapped) if rep == 0 else (swapped, grads)
        sides = jnp.concatenate([jnp.where(left, first, 0.0), jnp.where(left, 0.0, second)], axis=0)
        sent = jnp.dot(put, sides.astype(bf16), preferred_element_type=f32).astype(bf16)
        out_ref[rep * sent.shape[0] : (rep + 1) * sent.shape[0]] = sent
    margin_copy.wait()


def update_kernel(incoming_ref, mine_ref, other_ref, zt_ref, nt_ref, wt_ref, rt_ref, z_out, n_out, w_out):
    half = zt_ref.shape[0]
    incoming = incoming_ref[...]
    turned = incoming.T
    first = lax.axis_index("rep") == 0
    mine = jnp.dot(jnp.where(first, turned[:half], turned[half:]), mine_ref[...], preferred_element_type=f32)
    other = jnp.dot(jnp.where(first, turned[half:], turned[:half]), other_ref[...], preferred_element_type=f32)
    total = mine + other
    z_state = zt_ref[...]
    n_state = nt_ref[...]
    new_n = n_state + total * total
    sigma = (jnp.sqrt(new_n) - rt_ref[...]) / rate_alpha
    new_z = z_state + total - sigma * wt_ref[...]
    z_out[...] = new_z
    n_out[...] = new_n
    w_out[...] = shrink(new_z, new_n)


def call(kernel, out, specs, scratch=(), limit=16 << 20, flops=0, out_specs=None):
    return pl.pallas_call(
        kernel,
        out_shape=out,
        in_specs=specs,
        out_specs=jax.tree.map(lambda _: VMEM, out) if out_specs is None else out_specs,
        scratch_shapes=list(scratch),
        compiler_params=pltpu.CompilerParams(vmem_limit_bytes=limit),
        cost_estimate=pl.CostEstimate(flops=flops, bytes_accessed=0, transcendentals=0),
    )


def body(z_state, n_state, tile_values, tile_block, tile_group, labels):
    blk, lane = z_state.shape
    tiles = tile_block.shape[0]
    groups = labels.shape[0]
    shards = lax.axis_size("shard")
    reps = lax.axis_size("rep")
    half = lane // reps
    need = max(4, (tiles + shards - 2) // (shards - 1))
    lines = (need + 3) // 4 * 2
    devices = reps * shards
    parts = tiles // 128
    shape = jax.ShapeDtypeStruct
    in_hbm = functools.partial(pltpu.with_memory_space_constraint, memory_space=pltpu.HBM)

    def swap(x):
        return lax.all_to_all(x, ("rep", "shard"), split_axis=0, concat_axis=0, tiled=True)

    def swap_rows(x):
        return swap(x.reshape(devices, lines // 2, 2, lane)).reshape(x.shape)

    ids = tile_block.reshape(parts, 128)
    asked = swap(jnp.broadcast_to(ids[None], (devices, parts, 128)))
    pull, order, take, put, *state = call(
        functools.partial(prepare_kernel, shards, groups, lines),
        (
            shape((blk, lane), bf16),
            shape((1, tiles), i32),
            shape((tiles, devices * lines), bf16),
            shape((shards * lines, 2 * tiles), bf16),
        )
        + (shape((half, blk), f32),) * 4,
        [HBM] * 4,
        [pltpu.VMEM((parts, 128), i32)] * 2 + [pltpu.VMEM((blk, lane), f32)] * 2 + [pltpu.SemaphoreType.DMA((4,))],
        flops=4 * 10**9,
    )(*(in_hbm(x) for x in (ids, tile_group.reshape(parts, 128), z_state, n_state)))
    answer, mine = call(
        functools.partial(answer_kernel, lines),
        (shape((devices * lines, lane), bf16), shape((devices * lines, blk), bf16)),
        [VMEM] * 2,
        flops=8 * 10**9,
    )(asked, pull)
    margins, outgoing, other = call(
        functools.partial(worker_kernel, lines),
        (
            shape((groups, lane), f32),
            shape((devices * lines, lane), bf16),
            shape((devices * lines, blk), bf16),
        ),
        [VMEM] * 7,
        [
            pltpu.VMEM((tiles, lane), f32),
            pltpu.VMEM((tiles, lane), f32),
            pltpu.VMEM((groups, lane), f32),
            pltpu.SMEM((1, tiles), i32),
            pltpu.SemaphoreType.DMA((2,)),
        ],
        out_specs=(HBM, VMEM, VMEM),
    )(order, swap_rows(answer), take, put, labels, asked, tile_values)
    incoming = swap_rows(outgoing)
    outs = call(update_kernel, (shape((half, blk), f32),) * 3, [VMEM] * 7)(incoming, mine, other, *state)
    return (margins,) + tuple(o.T for o in outs)


def solution(mesh):
    placed = (
        P("shard", None),
        P("shard", None),
        P(("rep", "shard"), None, None),
        P(("rep", "shard")),
        P(("rep", "shard")),
        P(("rep", "shard"), None),
    )
    return jax.shard_map(
        body,
        mesh=mesh,
        in_specs=placed,
        out_specs=(
            P(("rep", "shard"), None),
            P("shard", "rep"),
            P("shard", "rep"),
            P("shard", "rep"),
        ),
        check_vma=False,
    )
```

```python
import functools

import jax
import jax.numpy as jnp
from jax import lax
from jax.experimental import pallas as pl
from jax.experimental.pallas import tpu as pltpu
from jax.sharding import PartitionSpec as P

rate_alpha = 0.5
rate_beta = 1.0
lasso_weight = 0.5
ridge_weight = 1.0

f32, bf16, i32 = jnp.float32, jnp.bfloat16, jnp.int32
VMEM = pl.BlockSpec(memory_space=pltpu.VMEM)
SMEM = pl.BlockSpec(memory_space=pltpu.SMEM)
HBM = pl.BlockSpec(memory_space=pltpu.HBM)


def shrink(z_acc, n_acc):
    soft = z_acc - jnp.clip(z_acc, -lasso_weight, lasso_weight)
    return -soft / ((rate_beta + jnp.sqrt(n_acc)) / rate_alpha + ridge_weight)


def iota(shape, dim):
    return lax.broadcasted_iota(i32, shape, dim)


def mask(hit):
    return hit.astype(f32).astype(bf16)


def before(size):
    return mask(iota((size, size), 0) < iota((size, size), 1))


def asked_slots(asked, first, blk):
    local = jnp.concatenate([asked[:, part, :] for part in range(asked.shape[1])], axis=1) - first
    valid = (local >= 0) & (local < blk)
    rank = jnp.dot(mask(valid), before(local.shape[1]), preferred_element_type=f32)
    return jnp.where(valid, rank, -1.0), jnp.where(valid, local, 0)


def slot_rows(rank, local, lines, *firsts):
    workers, tiles = rank.shape
    rows = workers * lines
    row = iota((rows, workers), 0)
    worker = iota((rows, workers), 1) * lines
    spread = mask((row >= worker) & (row < worker + lines))
    line = (iota((rows, tiles), 0) % lines).astype(f32)
    number = local + 1
    high = number // 256
    low = number - high * 256
    facts = jnp.concatenate([rank, high.astype(f32), low.astype(f32)], axis=1).astype(bf16)
    facts = jnp.dot(spread, facts, preferred_element_type=f32)
    each_rank = facts[:, :tiles]
    each = facts[:, tiles : 2 * tiles] * 256.0 + facts[:, 2 * tiles :]
    columns = []
    for first in firsts:
        picked = jnp.where(each_rank - first == line, each, 0.0)
        columns.append(jnp.sum(picked, axis=1, keepdims=True).astype(i32) - 1)
    return columns


def one_hot(column, blk):
    shape = (column.shape[0], 128)
    wide = jnp.broadcast_to(column, shape).astype(jnp.int16)
    one, zero = jnp.ones(shape, bf16), jnp.zeros(shape, bf16)
    parts = [jnp.where(wide == (iota(shape, 1) + at).astype(jnp.int16), one, zero) for at in range(0, blk, 128)]
    return jnp.concatenate(parts, axis=1)


def prepare_kernel(
    shards, groups, lines, block_hbm, group_hbm, z_hbm, n_hbm, pull_ref, order_ref, take_ref, put_ref, zt_ref, nt_ref,
    wt_ref, rt_ref,    block_ref, group_ref, z_ref, n_ref, sem
):
    copies = [
        pltpu.make_async_copy(source, target, sem.at[i])
        for i, (source, target) in enumerate(
            [(block_hbm, block_ref), (group_hbm, group_ref), (z_hbm, z_ref), (n_hbm, n_ref)]
        )
    ]
    for copy in copies:
        copy.start()
    copies[0].wait()
    copies[1].wait()
    blk, _ = z_ref.shape
    half = zt_ref.shape[0]
    parts = block_ref.shape[0]
    tiles = parts * 128
    rep = lax.axis_index("rep")
    tri = before(tiles)
    owner = jnp.concatenate([block_ref[i : i + 1] for i in range(parts)], axis=1) // blk
    group = jnp.concatenate([group_ref[i : i + 1] for i in range(parts)], axis=1)

    def rank_in(key, count):
        same = jnp.broadcast_to(key, (count, tiles)) == iota((count, tiles), 0)
        rank = jnp.dot(mask(same), tri, preferred_element_type=f32)
        return jnp.sum(jnp.where(same, rank, 0.0), axis=0, keepdims=True)

    rank = rank_in(owner, shards)
    place = (group * (tiles // groups)).astype(f32) + rank_in(group, groups)
    move = (jnp.broadcast_to(place.astype(i32), (tiles, tiles)) == iota((tiles, tiles), 0)).astype(f32)
    late = rank >= lines
    slot = owner.astype(f32) * lines + rank + jnp.where(late, (shards - 1) * lines * 1.0, 0.0)
    column = jnp.sum(move * slot, axis=1, keepdims=True).astype(i32)
    take_ref[...] = mask(jnp.broadcast_to(column, take_ref.shape) == iota(take_ref.shape, 1))
    row = iota((8, tiles), 0)
    facts = jnp.where(
        row == 0,
        jnp.broadcast_to(owner.astype(f32), (8, tiles)),
        jnp.where(row == 1, jnp.broadcast_to(rank, (8, tiles)), iota((8, tiles), 1).astype(f32)),
    )
    facts = lax.dot_general(
        facts.astype(bf16), move.astype(bf16), (((1,), (1,)), ((), ())), preferred_element_type=f32
    )
    order_ref[...] = facts[2:3].astype(i32)
    owner = facts[0:1].astype(i32)
    rank = facts[1:2].astype(i32)
    at = iota((shards * lines, tiles), 0)
    left = jnp.where(rank < lines, owner * lines + rank, -1)
    right = jnp.where(rank >= lines, owner * lines + rank - lines, -1)
    put_ref[:, :tiles] = mask(jnp.broadcast_to(left, at.shape) == at)
    put_ref[:, tiles:] = mask(jnp.broadcast_to(right, at.shape) == at)
    copies[2].wait()
    copies[3].wait()
    pull_ref[...] = shrink(z_ref[...], n_ref[...]).astype(bf16)
    zt = z_ref[...].T
    nt = n_ref[...].T
    zt = jnp.where(rep == 0, zt[:half], zt[half:])
    nt = jnp.where(rep == 0, nt[:half], nt[half:])
    zt_ref[...] = zt
    nt_ref[...] = nt
    wt_ref[...] = shrink(zt, nt)
    rt_ref[...] = jnp.sqrt(nt)


def answer_kernel(lines, asked_ref, pull_ref, answer_ref, hot_ref):
    blk, lane = pull_ref.shape
    me = lax.axis_index("shard")
    rep = lax.axis_index("rep")
    rank, local = asked_slots(asked_ref[...], me * blk, blk)
    (column,) = slot_rows(rank, local, lines, (rep * lines).astype(f32))
    hot = one_hot(column, blk)
    hot_ref[...] = hot
    answer_ref[...] = jnp.dot(hot, pull_ref[...], preferred_element_type=f32).astype(bf16)


def worker_kernel(
    lines, order_vmem, answer_ref, take_ref, put_ref, labels_ref, asked_ref, tile_ref, margin_hbm, out_ref, hot_ref,
    w_ref, grad_ref, margin_ref, order_ref, sem
):
    tiles, lane, _ = tile_ref.shape
    groups = labels_ref.shape[0]
    each = tiles // groups
    order_copy = pltpu.make_async_copy(order_vmem, order_ref, sem.at[0])
    margin_copy = pltpu.make_async_copy(margin_ref, margin_hbm, sem.at[1])
    order_copy.start()
    blk = hot_ref.shape[1]
    rank, local = asked_slots(asked_ref[...], lax.axis_index("shard") * blk, blk)
    other = (1 - lax.axis_index("rep")) * lines
    (column,) = slot_rows(rank, local, lines, other.astype(f32))
    hot_ref[...] = one_hot(column, blk)
    w_ref[...] = jnp.dot(take_ref[...], answer_ref[...], preferred_element_type=f32)
    order_copy.wait()
    resid = []
    for g in range(groups + 1):
        if g < groups:
            total = jnp.zeros((lane, lane), f32)
            whole = (g + 1) * each - 2
            for p in range(g * each, whole):
                total = total + tile_ref[order_ref[0, p]].astype(f32) * w_ref[p : p + 1, :]
            margin = jnp.sum(total, axis=1).reshape(1, lane)
            for p in range(whole, (g + 1) * each):
                weights = w_ref[p : p + 1, :].astype(bf16)
                margin = margin + lax.dot_general(
                    weights, tile_ref[order_ref[0, p]], (((1,), (1,)), ((), ())), preferred_element_type=f32
                )
            margin_ref[g : g + 1, :] = margin
            resid.append((jax.nn.sigmoid(margin) - labels_ref[g : g + 1, :].astype(f32)).astype(bf16))
        if g == groups - 1:
            margin_copy.start()
        if g > 0:
            for p in range((g - 1) * each, g * each, 2):
                pair = jnp.concatenate([tile_ref[order_ref[0, p]], tile_ref[order_ref[0, p + 1]]], axis=1)
                both = jnp.dot(resid[g - 1], pair, preferred_element_type=f32)
                grad_ref[p : p + 1, :] = both[:, :lane]
                grad_ref[p + 1 : p + 2, :] = both[:, lane:]
    grads = grad_ref[...]
    half = lane // 2
    swapped = jnp.concatenate([grads[:, half:], grads[:, :half]], axis=1)
    left = iota((tiles, lane), 1) < half
    put = put_ref[...]
    for rep in range(2):
        first, second = (grads, swapped) if rep == 0 else (swapped, grads)
        sides = jnp.concatenate([jnp.where(left, first, 0.0), jnp.where(left, 0.0, second)], axis=0)
        sent = jnp.dot(put, sides.astype(bf16), preferred_element_type=f32).astype(bf16)
        out_ref[rep * sent.shape[0] : (rep + 1) * sent.shape[0]] = sent
    margin_copy.wait()


def update_kernel(incoming_ref, mine_ref, other_ref, zt_ref, nt_ref, wt_ref, rt_ref, z_out, n_out, w_out):
    half = zt_ref.shape[0]
    incoming = incoming_ref[...]
    turned = incoming.T
    first = lax.axis_index("rep") == 0
    mine = jnp.dot(jnp.where(first, turned[:half], turned[half:]), mine_ref[...], preferred_element_type=f32)
    other = jnp.dot(jnp.where(first, turned[half:], turned[:half]), other_ref[...], preferred_element_type=f32)
    total = mine + other
    z_state = zt_ref[...]
    n_state = nt_ref[...]
    new_n = n_state + total * total
    sigma = (jnp.sqrt(new_n) - rt_ref[...]) / rate_alpha
    new_z = z_state + total - sigma * wt_ref[...]
    z_out[...] = new_z
    n_out[...] = new_n
    w_out[...] = shrink(new_z, new_n)


def call(kernel, out, specs, scratch=(), limit=16 << 20, flops=0, out_specs=None):
    return pl.pallas_call(
        kernel,
        out_shape=out,
        in_specs=specs,
        out_specs=jax.tree.map(lambda _: VMEM, out) if out_specs is None else out_specs,
        scratch_shapes=list(scratch),
        compiler_params=pltpu.CompilerParams(vmem_limit_bytes=limit),
        cost_estimate=pl.CostEstimate(flops=flops, bytes_accessed=0, transcendentals=0),
    )


def body(z_state, n_state, tile_values, tile_block, tile_group, labels):
    blk, lane = z_state.shape
    tiles = tile_block.shape[0]
    groups = labels.shape[0]
    shards = lax.axis_size("shard")
    reps = lax.axis_size("rep")
    half = lane // reps
    need = max(4, (tiles + shards - 2) // (shards - 1))
    lines = (need + 3) // 4 * 2
    devices = reps * shards
    parts = tiles // 128
    shape = jax.ShapeDtypeStruct
    in_hbm = functools.partial(pltpu.with_memory_space_constraint, memory_space=pltpu.HBM)

    def swap(x):
        return lax.all_to_all(x, ("rep", "shard"), split_axis=0, concat_axis=0, tiled=True)

    def swap_rows(x):
        return swap(x.reshape(devices, lines // 2, 2, lane)).reshape(x.shape)

    ids = tile_block.reshape(parts, 128)
    asked = swap(jnp.broadcast_to(ids[None], (devices, parts, 128)))
    pull, order, take, put, *state = call(
        functools.partial(prepare_kernel, shards, groups, lines),
        (
            shape((blk, lane), bf16),
            shape((1, tiles), i32),
            shape((tiles, devices * lines), bf16),
            shape((shards * lines, 2 * tiles), bf16),
        )
        + (shape((half, blk), f32),) * 4,
        [HBM] * 4,
        [pltpu.VMEM((parts, 128), i32)] * 2 + [pltpu.VMEM((blk, lane), f32)] * 2 + [pltpu.SemaphoreType.DMA((4,))],
        flops=4 * 10**9,
    )(*(in_hbm(x) for x in (ids, tile_group.reshape(parts, 128), z_state, n_state)))
    answer, mine = call(
        functools.partial(answer_kernel, lines),
        (shape((devices * lines, lane), bf16), shape((devices * lines, blk), bf16)),
        [VMEM] * 2,
        flops=8 * 10**9,
    )(asked, pull)
    margins, outgoing, other = call(
        functools.partial(worker_kernel, lines),
        (
            shape((groups, lane), f32),
            shape((devices * lines, lane), bf16),
            shape((devices * lines, blk), bf16),
        ),
        [VMEM] * 7,
        [
            pltpu.VMEM((tiles, lane), f32),
            pltpu.VMEM((tiles, lane), f32),
            pltpu.VMEM((groups, lane), f32),
            pltpu.SMEM((1, tiles), i32),
            pltpu.SemaphoreType.DMA((2,)),
        ],
        out_specs=(HBM, VMEM, VMEM),
    )(order, swap_rows(answer), take, put, labels, asked, tile_values)
    incoming = swap_rows(outgoing)
    outs = call(update_kernel, (shape((half, blk), f32),) * 3, [VMEM] * 7)(incoming, mine, other, *state)
    return (margins,) + tuple(o.T for o in outs)


def solution(mesh):
    placed = (
        P("shard", None),
        P("shard", None),
        P(("rep", "shard"), None, None),
        P(("rep", "shard")),
        P(("rep", "shard")),
        P(("rep", "shard"), None),
    )
    return jax.shard_map(
        body,
        mesh=mesh,
        in_specs=placed,
        out_specs=(
            P(("rep", "shard"), None),
            P("shard", "rep"),
            P("shard", "rep"),
            P("shard", "rep"),
        ),
        check_vma=False,
    )
```
